32 devices in a mesh: cells: 8 (over y, x, core), modes: 4 (over z).
Axes of the slice: x: 2, y: 2, z: 4, core: 2. Of those that a mesh axis runs over, the one named last changes fastest.
Arguments:
- phonons: float32 [8, 8, 8, 16, 6144], P('cells', None, None, None, 'modes'), may hold values from -6 to 6
- heaters: int32 [8, 8, 8, 16], P('cells'), may hold values 0 or 1
- courant: float32 [3, 6144], P(None, 'modes'), may hold values from 0.05 to 0.3
- upwind: int32 [3, 6144], P(None, 'modes'), may hold values from 0 to 1
- relaxation: float32 [6144], P('modes'), may hold values from 0.02 to 0.4
- source: float32 [6144], P('modes'), may hold values from -6 to 6
- coupling: bfloat16 [6144, 6144], P('modes'), may hold values from -0.0390625 to 0.0390625
Outputs:
- evolved: float32 [8, 8, 8, 16, 6144], P('cells', None, None, None, 'modes')
The draws below stay inside these ranges and needn't reach their ends.
All inputs are finite; a program needn't handle non-finite values. No bound on the sum of `heaters` on one device may be relied on, other than what follows from the above.
Results may differ from the reference program's by a relative error of at most 0.0018.
Values may be sent and summed in bfloat16 or wider, within the bound.
A program may use at most 128 MiB of HBM per device.

```python
import math
import jax
import jax.numpy as jnp
from jax import lax

MODES = 6144
GY = 4
CX = 8
CY = 8
CZ = 16
STEPS = 2
BLOCKS = 8


def with_ends(entries, key, low, high):
    longest = entries.shape.index(max(entries.shape))
    spots = []
    for shift in (0, 1):
        where = [jax.random.randint(jax.random.fold_in(key, axis), (), 0, length) for axis, length in enumerate(entries.shape)]
        where[longest] = (where[longest] + shift) % entries.shape[longest]
        spots.append(tuple(where))
    return entries.at[spots[0]].set(low).at[spots[1]].set(high)


def steps_of(rng, extent, pieces, smallest, top_value):
    def one(position, parts):
        draws = jax.random.uniform(jax.random.fold_in(jax.random.fold_in(rng, 6), position), (parts,), jnp.float32, smallest / len(pieces), top_value / len(pieces))
        return jnp.repeat(jnp.exp(draws), extent[position] // parts).reshape((-1,) + (1,) * (len(extent) - position - 1))

    level = one(*pieces[0])
    for cut in pieces[1:]:
        level = level * one(*cut)
    return level


def scatter_about(own_key, dims, spread, most, shards=(), dtype=jnp.bfloat16):
    loudness = steps_of(own_key, dims, shards, -0.22, 0.18) if shards else 1.0
    values = jax.random.normal(own_key, dims, jnp.float32) * spread * loudness
    return jnp.minimum(jnp.maximum(values, -most), most).astype(dtype)


def setup_inputs(seed: int = 0) -> dict:
    key_of = jax.random.split(jax.random.key(seed), 8)
    return {
        "phonons": scatter_about(key_of[0], (BLOCKS, CX, CY, CZ, MODES), 1.0, 6.0, ((0, 8), (4, 4)), jnp.float32),
        "heaters": with_ends((jax.random.randint(key_of[1], (BLOCKS, CX, CY, CZ), 0, 4) < 1).astype(jnp.int32), jax.random.fold_in(key_of[1], 1), 0, 1),
        "courant": jnp.clip(jnp.exp(math.log(0.3) - 1.7917595 * jax.random.uniform(key_of[2], (3, MODES), jnp.float32) ** steps_of(key_of[2], (3, MODES), ((1, 4),), -0.2, 0.2)), 0.05, 0.3),
        "upwind": with_ends(jax.random.randint(key_of[3], (3, MODES), 0, 2), jax.random.fold_in(key_of[3], 1), 0, 1).astype(jnp.int32),
        "relaxation": jnp.clip(jnp.exp(math.log(0.4) - 2.9957323 * jax.random.uniform(key_of[4], (MODES,), jnp.float32) ** steps_of(key_of[4], (MODES,), ((0, 4),), -0.2, 0.2)), 0.02, 0.4),
        "source": scatter_about(key_of[5], (MODES,), 1.0, 6.0, ((0, 4),), jnp.float32),
        "coupling": scatter_about(key_of[6], (MODES, MODES), (4 * MODES) ** -0.5, 0.0390625, ((0, 4),)),
    }


def to_grid(array, block_rows):
    placed = jnp.roll(array, 2, axis=0)
    shaped = placed.reshape((block_rows, GY) + array.shape[1:])
    order = (0, 2, 1, 3) + tuple(range(4, shaped.ndim))
    return shaped.transpose(order).reshape((block_rows * CX, GY * CY) + array.shape[3:])


def from_grid(grid, block_rows):
    shaped = grid.reshape((block_rows, CX, GY, CY) + grid.shape[2:])
    order = (0, 2, 1, 3) + tuple(range(4, shaped.ndim))
    blocks = shaped.transpose(order).reshape((block_rows * GY, CX, CY) + grid.shape[2:])
    return jnp.roll(blocks, -2, axis=0)


def upstream(density, forward, axis):
    widths = [(0, 0)] * density.ndim
    widths[axis] = (1, 1)
    padded = jnp.pad(density, widths)
    length_axis = density.shape[axis]
    behind = lax.slice_in_dim(padded, 0, length_axis, axis=axis)
    ahead = lax.slice_in_dim(padded, 2, length_axis + 2, axis=axis)
    return jnp.where(forward, behind, ahead)


def upstream_loop(density, forward, axis):
    behind = jnp.roll(density, 1, axis=axis)
    ahead = jnp.roll(density, -1, axis=axis)
    return jnp.where(forward, behind, ahead)


def reference(phonons, heaters, courant, upwind, relaxation, source, coupling):
    block_rows = phonons.shape[0] // GY
    density = to_grid(phonons, block_rows)
    heating = to_grid(heaters, block_rows).astype(jnp.float32)[..., None] * source
    widened = coupling.astype(jnp.float32)
    for repeat in range(STEPS):
        rounded = lax.optimization_barrier(density.astype(jnp.bfloat16)).astype(jnp.float32)
        scattered = jnp.dot(rounded.reshape(-1, MODES), widened.T, precision=lax.Precision.HIGHEST).reshape(density.shape)
        transport = courant[0] * (density - upstream_loop(density, upwind[0] == 1, 0))
        transport = transport + courant[1] * (density - upstream(density, upwind[1] == 1, 1))
        transport = transport + courant[2] * (density - upstream(density, upwind[2] == 1, 2))
        density = density - transport - relaxation * density - scattered + heating
    return from_grid(density, block_rows)
```

```python
import jax
import jax.numpy as jnp
from jax import lax
from jax.experimental import pallas as pl
from jax.experimental.pallas import tpu as pltpu
from jax.sharding import PartitionSpec as P

GY = 4
STEPS = 2

TILE = 768
SLOTS = 12
AHEAD = (3, 1)
PEER_AT = (0, 1, 2)
TWIN_AT = (2, 3, 6)
READY_AT = (4, 4, 8)
DRAIN = 4
MESH = pl.DeviceIdType.MESH


def line_kernel(phonons, heat, courant, upwind, relaxation, source, coupling, out, dens, own, got, weights, old,
                facex, facey, total, acc, rates, load_sem, ss, rs, fys, fyr, fxs, fxr, hs, hr, out_sem, credit):
    cell, me = lax.axis_index("cells"), lax.axis_index("modes")
    count, ny, nz, width = own.shape
    steps_all = STEPS * count
    rows = ny * nz
    blocks = lax.axis_size("cells")
    half = me // 2
    inner = lax.rem((me + 1) // 2, 2)
    is_inner = inner == 1
    is_outer = inner == 0
    toward = 1 - 2 * half
    inward, outward = me + toward, me - toward
    near, far = me + 2 * toward, 3 - 3 * half
    y_next, y_last = lax.rem(cell + 1, blocks), lax.rem(cell + blocks - 1, blocks)
    x_next, x_last = lax.rem(cell + GY, blocks), lax.rem(cell + blocks - GY, blocks)
    twin = cell + 1 - 2 * lax.rem(cell, 2)
    flip2 = 2 - 4 * lax.rem(cell // 2, 2)
    flip4 = 4 - 8 * lax.rem(cell // 4, 2)
    peers = (cell + flip2, cell + flip4, cell + flip2 + flip4)
    column = lax.rem(lax.rem(cell + 2, blocks), GY)
    low_ok = jnp.where(column != 0, 1.0, 0.0).astype(jnp.float32)
    high_ok = jnp.where(column != GY - 1, 1.0, 0.0).astype(jnp.float32)

    def remote(src, dst, send, recv, c, m):
        return pltpu.make_async_remote_copy(
            src_ref=src, dst_ref=dst, send_sem=send, recv_sem=recv, device_id=(c, m), device_id_type=MESH
        )

    def slot(i):
        return lax.rem(i, SLOTS)

    def own_in(i):
        return remote(
            own.at[lax.rem(i, count)], got.at[1 - inner, slot(i)], ss.at[0, i], rs.at[1 - inner, i], cell, inward
        )

    def own_out(i):
        return remote(own.at[lax.rem(i, count)], got.at[0, slot(i)], ss.at[1, i], rs.at[0, i], cell, outward)

    def relay(i):
        return remote(got.at[1, slot(i)], got.at[2, slot(i)], ss.at[2, i], rs.at[2, i], cell, inward)

    def part(i):
        return remote(got.at[1, slot(i)], got.at[2, slot(i)], ss.at[3, i], rs.at[2, i], cell, outward)

    def arrived(which, i):
        piece = got.at[which, slot(i)]
        remote(piece, piece, ss.at[0, i], rs.at[which, i], cell, inward).wait_recv()

    def face_y(side, i):
        line = own.at[lax.rem(i, count), ny - 1 if side == 0 else 0]
        return remote(line, facey.at[side, i], fys.at[side, i], fyr.at[side, i], y_next if side == 0 else y_last, me)

    def face_x(side, s):
        plane = own.at[count - 1 if side == 0 else 0]
        return remote(plane, facex.at[side, s], fxs.at[side, s], fxr.at[side, s], x_next if side == 0 else x_last, me)

    share = width // blocks

    def lent_rows(c):
        return pl.ds(pl.multiple_of(c * share, share), share)

    def lent_z(k):
        block = (near, far, inward)[k]
        src = coupling.at[lent_rows(cell), pl.ds(pl.multiple_of(block * width, width), width)]
        return remote(src, weights.at[4 + k, lent_rows(cell)], hs.at[k], hr.at[k], cell, inward)

    def lent_peer(q, k):
        piece = weights.at[4 + k, lent_rows(cell)]
        return remote(piece, piece, hs.at[3 + 3 * q + k], hr.at[3 + 3 * q + k], peers[q], me)

    def lent_twin(q, k):
        piece = weights.at[4 + k, lent_rows(cell if q == 3 else peers[q])]
        return remote(piece, piece, hs.at[12 + 3 * q + k], hr.at[12 + 3 * q + k], twin, me)

    def on_faces(i, act):
        act(face_y(0, i))
        act(face_y(1, i))
        pl.when(lax.rem(i, count) == 0)(lambda: act(face_x(1, i // count)))
        pl.when(lax.rem(i, count) == count - 1)(lambda: act(face_x(0, i // count)))

    def start_new(i):
        on_faces(i, lambda copy: copy.start())
        pl.when(is_outer)(lambda: own_in(i).start())

    def wait_sent(i):
        on_faces(i, lambda copy: copy.wait_send())
        own_in(i).wait_send()
        pl.when(jnp.logical_and(is_inner, i < count))(lambda: own_out(i).wait_send())

    def dot(piece, block, lanes):
        return lax.dot_general(
            piece[...].reshape(rows, width),
            weights[block, lanes, :],
            (((1,), (1,)), ((), ())),
            preferred_element_type=jnp.float32,
        )

    def tiles(body):
        @pl.loop(0, width // TILE)
        def _(tile):
            body(pl.ds(pl.multiple_of(tile * TILE, TILE), TILE))

    def send_part(i, value_of):
        relay(i).wait_send()
        lag = SLOTS - count
        pl.when(i >= lag)(lambda: part(i - lag).wait_send())

        def tile(lanes):
            value = value_of(lanes).astype(jnp.bfloat16)
            got[1, slot(i), :, :, lanes] = value.reshape(ny, nz, TILE)

        tiles(tile)
        part(i).start()

    def give_credit(i):
        @pl.when(i < steps_all - SLOTS)
        def _():
            pl.semaphore_signal(credit, inc=1, device_id=(cell, inward), device_id_type=MESH)

    def early_part(i):
        here = slot(i)
        send_part(i, lambda lanes: dot(got.at[0, here], 4, lanes) + dot(got.at[2, here], 5, lanes))
        give_credit(i)

    def inner_sums(i):
        s, k, here = i // count, lax.rem(i, count), slot(i)
        arrived(0, i)

        def first(lanes):
            total[:, lanes] = (
                dot(own.at[k], 0, lanes) + dot(got.at[0, here], 1, lanes) + dot(got.at[1, here], 2, lanes)
            )

        tiles(first)

        @pl.when(s >= 1)
        def _():
            def ahead(lanes):
                acc[:, lanes] = dot(own.at[k], 6, lanes) + dot(got.at[0, here], 4, lanes)

            tiles(ahead)

        arrived(2, i)

        @pl.when(s >= 1)
        def _():
            send_part(i, lambda lanes: acc[:, lanes] + dot(got.at[2, here], 5, lanes))

        def last(lanes):
            total[:, lanes] = total[:, lanes] + dot(got.at[2, here], 3, lanes)

        tiles(last)
        pl.when(s >= 1)(lambda: give_credit(i))

    def outer_sums(i):
        s, k, here = i // count, lax.rem(i, count), slot(i)

        def first(lanes):
            total[:, lanes] = dot(own.at[k], 0, lanes)

        tiles(first)

        @pl.when(s == 0)
        def _():
            arrived(0, i)

            def second(lanes):
                total[:, lanes] = total[:, lanes] + dot(got.at[0, here], 1, lanes)

            tiles(second)

        arrived(2, i)
        total[...] = total[...] + got[2, here].reshape(rows, width).astype(jnp.float32)

    def process(i):
        s, k = i // count, lax.rem(i, count)
        pl.when(is_inner)(lambda: inner_sums(i))
        pl.when(is_outer)(lambda: outer_sums(i))
        face_y(0, i).wait_recv()
        face_y(1, i).wait_recv()

        @pl.when(k == 0)
        def _():
            face_x(0, s).wait_recv()
            old[1, 1 : ny + 1] = facex[0, s].astype(jnp.float32)

        @pl.when(k == count - 1)
        def _():
            face_x(1, s).wait_recv()
            dens[count] = facex[1, s].astype(jnp.float32)

        wait_sent(i)
        spot = lax.broadcasted_iota(jnp.int32, (nz, 512), 0)
        diagonal = lax.broadcasted_iota(jnp.int32, (nz, nz), 0) == lax.broadcasted_iota(jnp.int32, (nz, nz), 1)
        cur = lax.rem(k, 2)
        old[cur, 1 : ny + 1] = dens[k]
        old[cur, 0] = facey[0, i].astype(jnp.float32) * low_ok
        old[cur, ny + 1] = facey[1, i].astype(jnp.float32) * high_ok

        @pl.loop(0, ny)
        def _(y):
            lit = heat[0, k, pl.ds(y, 1), :].astype(jnp.float32)
            warm = jnp.sum(jnp.where(diagonal, lit, 0.0), axis=1, keepdims=True)
            for lane in range(0, width, 512):
                lanes = slice(lane, lane + 512)
                here = old[cur, y + 1, :, lanes]
                new = rates[0:1, lanes] * here
                new += rates[1:2, lanes] * old[1 - cur, y + 1, :, lanes]
                new += rates[2:3, lanes] * dens[k + 1, y, :, lanes]
                new += rates[3:4, lanes] * old[cur, y, :, lanes]
                new += rates[4:5, lanes] * old[cur, y + 2, :, lanes]
                new += rates[5:6, lanes] * jnp.where(spot == 0, 0.0, pltpu.roll(here, 1, 0))
                new += rates[6:7, lanes] * jnp.where(spot == nz - 1, 0.0, pltpu.roll(here, nz - 1, 0))
                line = pl.ds(pl.multiple_of(y * nz, nz), nz)
                new += warm * rates[7:8, lanes] - total[line, lanes]
                dens[k, y, :, lanes] = new
                own[k, y, :, lanes] = new.astype(jnp.bfloat16)

        pl.when(s < STEPS - 1)(lambda: start_new(i + count))
        pl.when(s == STEPS - 1)(lambda: result(k).start())

    def result(k):
        return pltpu.make_async_copy(dens.at[k], out.at[0, k], out_sem.at[k])

    plane_loads = [pltpu.make_async_copy(phonons.at[0, k], dens.at[k], load_sem.at[4 + k]) for k in range(count)]
    for load in plane_loads:
        load.start()
    order = (me, inward, jnp.clip(outward, 0, 3), far)
    loads = [
        pltpu.make_async_copy(
            coupling.at[:, pl.ds(pl.multiple_of(block * width, width), width)], weights.at[j], load_sem.at[j]
        )
        for j, block in enumerate(order)
    ]
    barrier = pltpu.get_barrier_semaphore()

    def greet(c, m):
        pl.semaphore_signal(barrier, inc=1, device_id=(c, m), device_id_type=MESH)

    greet(cell, inward)
    pl.when(is_inner)(lambda: greet(cell, outward))
    for c in (y_next, y_last, x_next, x_last, twin) + peers:
        greet(c, me)
    for load in loads:
        load.start()
    stay = 1.0 - courant[0:1] - courant[1:2] - courant[2:3] - relaxation[...].reshape(1, width)
    rates[0:1] = stay
    for d in range(3):
        speed = courant[d : d + 1]
        forward = upwind[d : d + 1] == 1
        rates[1 + 2 * d : 2 + 2 * d] = jnp.where(forward, speed, 0.0)
        rates[2 + 2 * d : 3 + 2 * d] = jnp.where(forward, 0.0, speed)
    rates[7:8] = source[...].reshape(1, width)
    pl.semaphore_wait(barrier, 9 + inner)

    @pl.when(is_outer)
    def _():
        lent_z(0).start()
        lent_z(1).start()

    for i in range(count):
        plane_loads[i].wait()
        own[i] = dens[i].astype(jnp.bfloat16)
        start_new(jnp.int32(i))

        @pl.when(is_inner)
        def _():
            if i < AHEAD[0]:
                own_in(jnp.int32(i)).start()
            own_out(jnp.int32(i)).start()

        if i == 1:
            pl.when(is_outer)(lambda: lent_z(2).start())

    @pl.loop(0, steps_all + 1)
    def _(t):
        @pl.when(is_inner)
        def _():
            @pl.when(t < steps_all)
            def _():
                arrived(1, t)
                relay(t).start()

            pl.when(t + AHEAD[0] < count)(lambda: own_in(t + AHEAD[0]).start())

            @pl.when(jnp.logical_and(t + AHEAD[1] >= count, t + AHEAD[1] < steps_all))
            def _():
                pl.when(t + AHEAD[1] >= SLOTS)(lambda: pl.semaphore_wait(credit, 1))
                own_in(t + AHEAD[1]).start()

            for k in range(3):

                @pl.when(t == PEER_AT[k])
                def _():
                    lent_z(k).wait_recv()
                    for q in range(3):
                        lent_peer(q, k).start()

                @pl.when(t == TWIN_AT[k])
                def _():
                    for q in range(3):
                        lent_peer(q, k).wait_recv()
                    for q in range(4):
                        lent_twin(q, k).start()

                @pl.when(t == READY_AT[k])
                def _():
                    for q in range(4):
                        lent_twin(q, k).wait_recv()

        @pl.when(t == 1)
        def _():
            for load in loads:
                load.wait()

        @pl.when(t >= 1)
        def _():
            u = t - 1
            process(u)

            @pl.when(jnp.logical_and(is_inner, u >= DRAIN))
            def _():
                for extra in range(2):
                    late = 2 * (u - DRAIN) + extra
                    pl.when(late < count)(lambda: early_part(late))

    @pl.loop(0, count)
    def _(k):
        result(k).wait()

    @pl.when(is_inner)
    def _():
        for i in range(steps_all - (SLOTS - count), steps_all):
            part(jnp.int32(i)).wait_send()
        for k in range(3):
            for q in range(3):
                lent_peer(q, k).wait_send()
            for q in range(4):
                lent_twin(q, k).wait_send()

    @pl.when(is_outer)
    def _():
        for k in range(3):
            lent_z(k).wait_send()


def line_device(phonons, heaters, courant, upwind, relaxation, source, coupling):
    _, count, ny, nz, width = phonons.shape
    calls = STEPS * count
    anywhere, vmem = pl.BlockSpec(memory_space=pl.ANY), pl.BlockSpec(memory_space=pltpu.VMEM)
    dma = pltpu.SemaphoreType.DMA
    half, full = jnp.bfloat16, jnp.float32
    return pl.pallas_call(
        line_kernel,
        out_shape=jax.ShapeDtypeStruct(phonons.shape, full),
        in_specs=[anywhere, vmem, vmem, vmem, vmem, vmem, anywhere],
        out_specs=anywhere,
        scratch_shapes=[
            pltpu.VMEM((count + 1, ny, nz, width), full),
            pltpu.VMEM((count, ny, nz, width), half),
            pltpu.VMEM((3, SLOTS, ny, nz, width), half),
            pltpu.VMEM((7, width, width), half),
            pltpu.VMEM((2, ny + 2, nz, width), full),
            pltpu.VMEM((2, STEPS, ny, nz, width), half),
            pltpu.VMEM((2, calls, nz, width), half),
            pltpu.VMEM((ny * nz, width), full),
            pltpu.VMEM((ny * nz, width), full),
            pltpu.VMEM((8, width), full),
            dma((4 + count,)),
            dma((4, calls)),
            dma((3, calls)),
            dma((2, calls)),
            dma((2, calls)),
            dma((2, STEPS)),
            dma((2, STEPS)),
            dma((24,)),
            dma((24,)),
            dma((count,)),
            pltpu.SemaphoreType.REGULAR,
        ],
        compiler_params=pltpu.CompilerParams(
            collective_id=0, has_side_effects=True, vmem_limit_bytes=64 * 2**20 - 2**18
        ),
    )(phonons, heaters, courant, upwind, relaxation, source, coupling)


def shifted(block, axis, distance):
    devices = range(lax.axis_size(axis))
    route = [((i - distance) % len(devices), i) for i in devices]
    return lax.ppermute(block, axis, route)


def upstream(density, forward, axis):
    widths = [(0, 0)] * density.ndim
    widths[axis] = (1, 1)
    padded = jnp.pad(density, widths)
    length_axis = density.shape[axis]
    behind = lax.slice_in_dim(padded, 0, length_axis, axis=axis)
    ahead = lax.slice_in_dim(padded, 2, length_axis + 2, axis=axis)
    return jnp.where(forward, behind, ahead)


def scatter_term(rounded, coupling):
    contract = (((1,), (1,)), ((), ()))
    gathered = lax.all_gather(rounded, "modes", axis=1, tiled=True)
    return lax.dot_general(gathered, coupling, contract, preferred_element_type=jnp.float32)


def advect(density, courant, upwind, masks):
    lower_y_ok, upper_y_ok = masks
    forward_x = upwind[0] == 1
    forward_y = upwind[1] == 1
    forward_z = upwind[2] == 1
    below_x = shifted(density[-1].astype(jnp.bfloat16), "cells", GY).astype(jnp.float32)
    above_x = shifted(density[0], "cells", -GY)
    below_y = (
        shifted(density[:, -1].astype(jnp.bfloat16), "cells", 1).astype(jnp.float32) * lower_y_ok
    )
    above_y = (
        shifted(density[:, 0].astype(jnp.bfloat16), "cells", -1).astype(jnp.float32) * upper_y_ok
    )
    upstream_z = upstream(density, forward_z, 2)
    transport = courant[0] * (density - upstream(density, forward_x, 0))
    transport = transport + courant[1] * (density - upstream(density, forward_y, 1))
    transport = transport + courant[2] * (density - upstream_z)
    transport = transport.at[0].add(-courant[0] * jnp.where(forward_x, below_x, 0.0))
    transport = transport.at[-1].add(-courant[0] * jnp.where(forward_x, 0.0, above_x))
    transport = transport.at[:, 0].add(-courant[1] * jnp.where(forward_y, below_y, 0.0))
    transport = transport.at[:, -1].add(-courant[1] * jnp.where(forward_y, 0.0, above_y))
    return transport


def per_device(phonons, heaters, courant, upwind, relaxation, source, coupling):
    density = phonons[0]
    cell_count = density.shape[0] * density.shape[1] * density.shape[2]
    mode_count = density.shape[3]
    block_total = lax.axis_size("cells")
    position = (lax.axis_index("cells") + 2) % block_total
    column = position % GY
    masks = ((column != 0).astype(jnp.float32), (column != GY - 1).astype(jnp.float32))
    heating = heaters[0].astype(jnp.float32)[..., None] * source
    for repeat in range(STEPS):
        rounded = density.astype(jnp.bfloat16).reshape(cell_count, mode_count)
        scattered = scatter_term(rounded, coupling).reshape(density.shape)
        transport = advect(density, courant, upwind, masks)
        density = density - transport - relaxation * density - scattered + heating
    return density[None]


def solution(mesh):
    placed = (
        P("cells", None, None, None, "modes"),
        P("cells", None, None, None),
        P(None, "modes"),
        P(None, "modes"),
        P("modes"),
        P("modes"),
        P("modes", None),
    )
    on_line = mesh.shape["modes"] == 4 and mesh.shape["cells"] == 8
    return jax.shard_map(
        line_device if on_line else per_device,
        mesh=mesh,
        in_specs=placed,
        out_specs=P("cells", None, None, None, "modes"),
        check_vma=False,
    )
```

```python
import jax
import jax.numpy as jnp
from jax import lax
from jax.experimental import pallas as pl
from jax.experimental.pallas import tpu as pltpu
from jax.sharding import PartitionSpec as P

GY = 4
STEPS = 2

TILE = 768
SLOTS = 12
AHEAD = (3, 1)
PEER_AT = (1, 2, 4)
TWIN_AT = (3, 4, 6)
READY_AT = (5, 5, 8)
LENT_AFTER = (1, 2, 4)
DRAIN = 4
MESH = pl.DeviceIdType.MESH


def line_kernel(phonons, heat, courant, upwind, relaxation, source, coupling, out, above, own, got, weights, old,
                facex, facey, total, acc, rates, load_sem, ss, rs, fys, fyr, fxs, fxr, hs, hr, credit):
    cell, me = lax.axis_index("cells"), lax.axis_index("modes")
    count, ny, nz, width = own.shape
    dens = out.at[0]
    steps_all = STEPS * count
    rows = ny * nz
    blocks = lax.axis_size("cells")
    half = me // 2
    inner = lax.rem((me + 1) // 2, 2)
    is_inner = inner == 1
    is_outer = inner == 0
    toward = 1 - 2 * half
    inward, outward = me + toward, me - toward
    near, far = me + 2 * toward, 3 - 3 * half
    y_next, y_last = lax.rem(cell + 1, blocks), lax.rem(cell + blocks - 1, blocks)
    x_next, x_last = lax.rem(cell + GY, blocks), lax.rem(cell + blocks - GY, blocks)
    twin = cell + 1 - 2 * lax.rem(cell, 2)
    flip2 = 2 - 4 * lax.rem(cell // 2, 2)
    flip4 = 4 - 8 * lax.rem(cell // 4, 2)
    peers = (cell + flip2, cell + flip4, cell + flip2 + flip4)
    column = lax.rem(lax.rem(cell + 2, blocks), GY)
    low_ok = jnp.where(column != 0, 1.0, 0.0).astype(jnp.float32)
    high_ok = jnp.where(column != GY - 1, 1.0, 0.0).astype(jnp.float32)

    def remote(src, dst, send, recv, c, m):
        return pltpu.make_async_remote_copy(
            src_ref=src, dst_ref=dst, send_sem=send, recv_sem=recv, device_id=(c, m), device_id_type=MESH
        )

    def slot(i):
        return lax.rem(i, SLOTS)

    def own_in(i):
        return remote(
            own.at[lax.rem(i, count)], got.at[1 - inner, slot(i)], ss.at[0, i], rs.at[1 - inner, i], cell, inward
        )

    def own_out(i):
        return remote(own.at[lax.rem(i, count)], got.at[0, slot(i)], ss.at[1, i], rs.at[0, i], cell, outward)

    def relay(i):
        return remote(got.at[1, slot(i)], got.at[2, slot(i)], ss.at[2, i], rs.at[2, i], cell, inward)

    def part(i):
        return remote(got.at[1, slot(i)], got.at[2, slot(i)], ss.at[3, i], rs.at[2, i], cell, outward)

    def arrived(which, i):
        piece = got.at[which, slot(i)]
        remote(piece, piece, ss.at[0, i], rs.at[which, i], cell, inward).wait_recv()

    def face_y(side, i):
        line = own.at[lax.rem(i, count), ny - 1 if side == 0 else 0]
        return remote(line, facey.at[side, i], fys.at[side, i], fyr.at[side, i], y_next if side == 0 else y_last, me)

    def face_x(side, s):
        plane = own.at[count - 1 if side == 0 else 0]
        return remote(plane, facex.at[side, s], fxs.at[side, s], fxr.at[side, s], x_next if side == 0 else x_last, me)

    share = width // blocks

    def lent_rows(c):
        return pl.ds(pl.multiple_of(c * share, share), share)

    def lent_z(k):
        block = (near, far, inward)[k]
        src = coupling.at[lent_rows(cell), pl.ds(pl.multiple_of(block * width, width), width)]
        return remote(src, weights.at[4 + k, lent_rows(cell)], hs.at[k], hr.at[k], cell, inward)

    def lent_peer(q, k):
        piece = weights.at[4 + k, lent_rows(cell)]
        return remote(piece, piece, hs.at[3 + 3 * q + k], hr.at[3 + 3 * q + k], peers[q], me)

    def lent_twin(q, k):
        piece = weights.at[4 + k, lent_rows(cell if q == 3 else peers[q])]
        return remote(piece, piece, hs.at[12 + 3 * q + k], hr.at[12 + 3 * q + k], twin, me)

    def on_faces(i, act):
        act(face_y(0, i))
        act(face_y(1, i))
        pl.when(lax.rem(i, count) == 0)(lambda: act(face_x(1, i // count)))
        pl.when(lax.rem(i, count) == count - 1)(lambda: act(face_x(0, i // count)))

    def start_new(i):
        on_faces(i, lambda copy: copy.start())
        pl.when(is_outer)(lambda: own_in(i).start())

    def wait_sent(i):
        on_faces(i, lambda copy: copy.wait_send())
        own_in(i).wait_send()
        pl.when(jnp.logical_and(is_inner, i < count))(lambda: own_out(i).wait_send())

    def dot(piece, block, lanes):
        return lax.dot_general(
            piece[...].reshape(rows, width),
            weights[block, lanes, :],
            (((1,), (1,)), ((), ())),
            preferred_element_type=jnp.float32,
        )

    def tiles(body):
        @pl.loop(0, width // TILE)
        def _(tile):
            body(pl.ds(pl.multiple_of(tile * TILE, TILE), TILE))

    def send_part(i, value_of):
        relay(i).wait_send()
        lag = SLOTS - count
        pl.when(i >= lag)(lambda: part(i - lag).wait_send())

        def tile(lanes):
            value = value_of(lanes).astype(jnp.bfloat16)
            got[1, slot(i), :, :, lanes] = value.reshape(ny, nz, TILE)

        tiles(tile)
        part(i).start()

    def give_credit(i):
        @pl.when(i < steps_all - SLOTS)
        def _():
            pl.semaphore_signal(credit, inc=1, device_id=(cell, inward), device_id_type=MESH)

    def early_part(i):
        here = slot(i)
        send_part(i, lambda lanes: dot(got.at[0, here], 4, lanes) + dot(got.at[2, here], 5, lanes))
        give_credit(i)

    def late_part(i):
        here = slot(i)
        send_part(i, lambda lanes: acc[:, lanes] + dot(got.at[2, here], 5, lanes))

    def inner_sums(i):
        s, k, here = i // count, lax.rem(i, count), slot(i)
        arrived(0, i)

        def first(lanes):
            total[:, lanes] = (
                dot(own.at[k], 0, lanes) + dot(got.at[0, here], 1, lanes) + dot(got.at[1, here], 2, lanes)
            )

        tiles(first)

        @pl.when(s >= 1)
        def _():
            def ahead(lanes):
                acc[:, lanes] = dot(own.at[k], 6, lanes) + dot(got.at[0, here], 4, lanes)

            tiles(ahead)

    def outer_sums(i):
        s, k, here = i // count, lax.rem(i, count), slot(i)

        def first(lanes):
            total[:, lanes] = dot(own.at[k], 0, lanes)

        tiles(first)

        @pl.when(s == 0)
        def _():
            arrived(0, i)

            def second(lanes):
                total[:, lanes] = total[:, lanes] + dot(got.at[0, here], 1, lanes)

            tiles(second)

    def process(i):
        s, k = i // count, lax.rem(i, count)
        pl.when(is_inner)(lambda: inner_sums(i))
        pl.when(is_outer)(lambda: outer_sums(i))
        face_y(0, i).wait_recv()
        face_y(1, i).wait_recv()

        @pl.when(k == 0)
        def _():
            face_x(0, s).wait_recv()
            old[1, 1 : ny + 1] = facex[0, s].astype(jnp.float32)

        @pl.when(k < count - 1)
        def _():
            above[...] = dens[k + 1]

        @pl.when(k == count - 1)
        def _():
            face_x(1, s).wait_recv()
            above[...] = facex[1, s].astype(jnp.float32)

        spot = lax.broadcasted_iota(jnp.int32, (nz, 512), 0)
        diagonal = lax.broadcasted_iota(jnp.int32, (nz, nz), 0) == lax.broadcasted_iota(jnp.int32, (nz, nz), 1)
        cur = lax.rem(k, 2)
        old[cur, 1 : ny + 1] = dens[k]
        old[cur, 0] = facey[0, i].astype(jnp.float32) * low_ok
        old[cur, ny + 1] = facey[1, i].astype(jnp.float32) * high_ok

        @pl.loop(0, ny)
        def _(y):
            lit = heat[0, k, pl.ds(y, 1), :].astype(jnp.float32)
            warm = jnp.sum(jnp.where(diagonal, lit, 0.0), axis=1, keepdims=True)
            for lane in range(0, width, 512):
                lanes = slice(lane, lane + 512)
                here = old[cur, y + 1, :, lanes]
                new = rates[0:1, lanes] * here
                new += rates[1:2, lanes] * old[1 - cur, y + 1, :, lanes]
                new += rates[2:3, lanes] * above[y, :, lanes]
                new += rates[3:4, lanes] * old[cur, y, :, lanes]
                new += rates[4:5, lanes] * old[cur, y + 2, :, lanes]
                new += rates[5:6, lanes] * jnp.where(spot == 0, 0.0, pltpu.roll(here, 1, 0))
                new += rates[6:7, lanes] * jnp.where(spot == nz - 1, 0.0, pltpu.roll(here, nz - 1, 0))
                line = pl.ds(pl.multiple_of(y * nz, nz), nz)
                total[line, lanes] = new + warm * rates[7:8, lanes] - total[line, lanes]

        arrived(2, i)
        pl.when(jnp.logical_and(is_inner, s >= 1))(lambda: late_part(i))
        wait_sent(i)
        here = slot(i)

        def finish(lanes, last):
            new = (total[:, lanes] - last).reshape(ny, nz, TILE)
            dens[k, :, :, lanes] = new
            own[k, :, :, lanes] = new.astype(jnp.bfloat16)

        @pl.when(is_inner)
        def _():
            tiles(lambda lanes: finish(lanes, dot(got.at[2, here], 3, lanes)))
            pl.when(s >= 1)(lambda: give_credit(i))

        @pl.when(is_outer)
        def _():
            tiles(lambda lanes: finish(lanes, got[2, here, :, :, lanes].reshape(rows, TILE).astype(jnp.float32)))

        pl.when(s < STEPS - 1)(lambda: start_new(i + count))

    plane_loads = [pltpu.make_async_copy(phonons.at[0, k], dens.at[k], load_sem.at[4 + k]) for k in range(count)]
    for load in plane_loads:
        load.start()
    order = (me, inward, jnp.clip(outward, 0, 3), far)
    loads = [
        pltpu.make_async_copy(
            coupling.at[:, pl.ds(pl.multiple_of(block * width, width), width)], weights.at[j], load_sem.at[j]
        )
        for j, block in enumerate(order)
    ]
    barrier = pltpu.get_barrier_semaphore()

    def greet(c, m):
        pl.semaphore_signal(barrier, inc=1, device_id=(c, m), device_id_type=MESH)

    greet(cell, inward)
    pl.when(is_inner)(lambda: greet(cell, outward))
    for c in (y_next, y_last, x_next, x_last, twin) + peers:
        greet(c, me)
    for load in loads:
        load.start()
    stay = 1.0 - courant[0:1] - courant[1:2] - courant[2:3] - relaxation[...].reshape(1, width)
    rates[0:1] = stay
    for d in range(3):
        speed = courant[d : d + 1]
        forward = upwind[d : d + 1] == 1
        rates[1 + 2 * d : 2 + 2 * d] = jnp.where(forward, speed, 0.0)
        rates[2 + 2 * d : 3 + 2 * d] = jnp.where(forward, 0.0, speed)
    rates[7:8] = source[...].reshape(1, width)
    pl.semaphore_wait(barrier, 9 + inner)

    for i in range(count):
        plane_loads[i].wait()
        own[i] = dens[i].astype(jnp.bfloat16)
        start_new(jnp.int32(i))

        @pl.when(is_inner)
        def _():
            if i < AHEAD[0]:
                own_in(jnp.int32(i)).start()
            own_out(jnp.int32(i)).start()

        if i in LENT_AFTER:
            pl.when(is_outer)(lambda: lent_z(LENT_AFTER.index(i)).start())

    @pl.loop(0, steps_all + 1)
    def _(t):
        @pl.when(is_inner)
        def _():
            @pl.when(t < steps_all)
            def _():
                arrived(1, t)
                relay(t).start()

            pl.when(t + AHEAD[0] < count)(lambda: own_in(t + AHEAD[0]).start())

            @pl.when(jnp.logical_and(t + AHEAD[1] >= count, t + AHEAD[1] < steps_all))
            def _():
                pl.when(t + AHEAD[1] >= SLOTS)(lambda: pl.semaphore_wait(credit, 1))
                own_in(t + AHEAD[1]).start()

            for k in range(3):

                @pl.when(t == PEER_AT[k])
                def _():
                    lent_z(k).wait_recv()
                    for q in range(3):
                        lent_peer(q, k).start()

                @pl.when(t == TWIN_AT[k])
                def _():
                    for q in range(3):
                        lent_peer(q, k).wait_recv()
                    for q in range(4):
                        lent_twin(q, k).start()

                @pl.when(t == READY_AT[k])
                def _():
                    for q in range(4):
                        lent_twin(q, k).wait_recv()

        @pl.when(t == 1)
        def _():
            for load in loads:
                load.wait()

        @pl.when(t >= 1)
        def _():
            u = t - 1
            process(u)

            @pl.when(jnp.logical_and(is_inner, u >= DRAIN))
            def _():
                for extra in range(2):
                    late = 2 * (u - DRAIN) + extra
                    pl.when(late < count)(lambda: early_part(late))

    @pl.when(is_inner)
    def _():
        for i in range(steps_all - (SLOTS - count), steps_all):
            part(jnp.int32(i)).wait_send()
        for k in range(3):
            for q in range(3):
                lent_peer(q, k).wait_send()
            for q in range(4):
                lent_twin(q, k).wait_send()

    @pl.when(is_outer)
    def _():
        for k in range(3):
            lent_z(k).wait_send()


def line_device(phonons, heaters, courant, upwind, relaxation, source, coupling):
    _, count, ny, nz, width = phonons.shape
    calls = STEPS * count
    anywhere, vmem = pl.BlockSpec(memory_space=pl.ANY), pl.BlockSpec(memory_space=pltpu.VMEM)
    dma = pltpu.SemaphoreType.DMA
    half, full = jnp.bfloat16, jnp.float32
    return pl.pallas_call(
        line_kernel,
        out_shape=pltpu.VMEM(phonons.shape, full),
        in_specs=[anywhere, vmem, vmem, vmem, vmem, vmem, anywhere],
        out_specs=vmem,
        scratch_shapes=[
            pltpu.VMEM((ny, nz, width), full),
            pltpu.VMEM((count, ny, nz, width), half),
            pltpu.VMEM((3, SLOTS, ny, nz, width), half),
            pltpu.VMEM((7, width, width), half),
            pltpu.VMEM((2, ny + 2, nz, width), full),
            pltpu.VMEM((2, STEPS, ny, nz, width), half),
            pltpu.VMEM((2, calls, nz, width), half),
            pltpu.VMEM((ny * nz, width), full),
            pltpu.VMEM((ny * nz, width), full),
            pltpu.VMEM((8, width), full),
            dma((4 + count,)),
            dma((4, calls)),
            dma((3, calls)),
            dma((2, calls)),
            dma((2, calls)),
            dma((2, STEPS)),
            dma((2, STEPS)),
            dma((24,)),
            dma((24,)),
            pltpu.SemaphoreType.REGULAR,
        ],
        compiler_params=pltpu.CompilerParams(
            collective_id=0, has_side_effects=True, vmem_limit_bytes=64 * 2**20 - 2**18 - 4 * phonons.size
        ),
    )(phonons, heaters, courant, upwind, relaxation, source, coupling)


def shifted(block, axis, distance):
    devices = range(lax.axis_size(axis))
    route = [((i - distance) % len(devices), i) for i in devices]
    return lax.ppermute(block, axis, route)


def upstream(density, forward, axis):
    widths = [(0, 0)] * density.ndim
    widths[axis] = (1, 1)
    padded = jnp.pad(density, widths)
    length_axis = density.shape[axis]
    behind = lax.slice_in_dim(padded, 0, length_axis, axis=axis)
    ahead = lax.slice_in_dim(padded, 2, length_axis + 2, axis=axis)
    return jnp.where(forward, behind, ahead)


def scatter_term(rounded, coupling):
    contract = (((1,), (1,)), ((), ()))
    gathered = lax.all_gather(rounded, "modes", axis=1, tiled=True)
    return lax.dot_general(gathered, coupling, contract, preferred_element_type=jnp.float32)


def advect(density, courant, upwind, masks):
    lower_y_ok, upper_y_ok = masks
    forward_x = upwind[0] == 1
    forward_y = upwind[1] == 1
    forward_z = upwind[2] == 1
    below_x = shifted(density[-1].astype(jnp.bfloat16), "cells", GY).astype(jnp.float32)
    above_x = shifted(density[0], "cells", -GY)
    below_y = (
        shifted(density[:, -1].astype(jnp.bfloat16), "cells", 1).astype(jnp.float32) * lower_y_ok
    )
    above_y = (
        shifted(density[:, 0].astype(jnp.bfloat16), "cells", -1).astype(jnp.float32) * upper_y_ok
    )
    upstream_z = upstream(density, forward_z, 2)
    transport = courant[0] * (density - upstream(density, forward_x, 0))
    transport = transport + courant[1] * (density - upstream(density, forward_y, 1))
    transport = transport + courant[2] * (density - upstream_z)
    transport = transport.at[0].add(-courant[0] * jnp.where(forward_x, below_x, 0.0))
    transport = transport.at[-1].add(-courant[0] * jnp.where(forward_x, 0.0, above_x))
    transport = transport.at[:, 0].add(-courant[1] * jnp.where(forward_y, below_y, 0.0))
    transport = transport.at[:, -1].add(-courant[1] * jnp.where(forward_y, 0.0, above_y))
    return transport


def per_device(phonons, heaters, courant, upwind, relaxation, source, coupling):
    density = phonons[0]
    cell_count = density.shape[0] * density.shape[1] * density.shape[2]
    mode_count = density.shape[3]
    block_total = lax.axis_size("cells")
    position = (lax.axis_index("cells") + 2) % block_total
    column = position % GY
    masks = ((column != 0).astype(jnp.float32), (column != GY - 1).astype(jnp.float32))
    heating = heaters[0].astype(jnp.float32)[..., None] * source
    for repeat in range(STEPS):
        rounded = density.astype(jnp.bfloat16).reshape(cell_count, mode_count)
        scattered = scatter_term(rounded, coupling).reshape(density.shape)
        transport = advect(density, courant, upwind, masks)
        density = density - transport - relaxation * density - scattered + heating
    return density[None]


def solution(mesh):
    placed = (
        P("cells", None, None, None, "modes"),
        P("cells", None, None, None),
        P(None, "modes"),
        P(None, "modes"),
        P("modes"),
        P("modes"),
        P("modes", None),
    )
    on_line = mesh.shape["modes"] == 4 and mesh.shape["cells"] == 8
    return jax.shard_map(
        line_device if on_line else per_device,
        mesh=mesh,
        in_specs=placed,
        out_specs=P("cells", None, None, None, "modes"),
        check_vma=False,
    )
```

```python
import jax
import jax.numpy as jnp
from jax import lax
from jax.experimental import pallas as pl
from jax.experimental.pallas import tpu as pltpu
from jax.sharding import PartitionSpec as P

GY = 4
STEPS = 2

TILE = 768
SLOTS = 12
AHEAD = (3, 1)
PEER_AT = (1, 2, 4)
TWIN_AT = (3, 4, 6)
READY_AT = (5, 5, 8)
LENT_AFTER = (1, 2, 4)
DRAIN = 4
CUTS = 4
MESH = pl.DeviceIdType.MESH


def line_kernel(phonons, heat, courant, upwind, relaxation, source, coupling, out, above, own, got, weights, old,
                facex, facey, total, acc, rates, load_sem, ss, rs, fys, fyr, fxs, fxr, hs, hr, cut_send, cut_recv, credit):
    cell, me = lax.axis_index("cells"), lax.axis_index("modes")
    count, ny, nz, width = own.shape
    dens = out.at[0]
    steps_all = STEPS * count
    last, final = steps_all - 1, (steps_all - 1) % SLOTS
    span = ny // CUTS
    rows = ny * nz
    blocks = lax.axis_size("cells")
    half = me // 2
    inner = lax.rem((me + 1) // 2, 2)
    is_inner = inner == 1
    is_outer = inner == 0
    toward = 1 - 2 * half
    inward, outward = me + toward, me - toward
    near, far = me + 2 * toward, 3 - 3 * half
    y_next, y_last = lax.rem(cell + 1, blocks), lax.rem(cell + blocks - 1, blocks)
    x_next, x_last = lax.rem(cell + GY, blocks), lax.rem(cell + blocks - GY, blocks)
    twin = cell + 1 - 2 * lax.rem(cell, 2)
    flip2 = 2 - 4 * lax.rem(cell // 2, 2)
    flip4 = 4 - 8 * lax.rem(cell // 4, 2)
    peers = (cell + flip2, cell + flip4, cell + flip2 + flip4)
    column = lax.rem(lax.rem(cell + 2, blocks), GY)
    low_ok = jnp.where(column != 0, 1.0, 0.0).astype(jnp.float32)
    high_ok = jnp.where(column != GY - 1, 1.0, 0.0).astype(jnp.float32)

    def remote(src, dst, send, recv, c, m):
        return pltpu.make_async_remote_copy(
            src_ref=src, dst_ref=dst, send_sem=send, recv_sem=recv, device_id=(c, m), device_id_type=MESH
        )

    def slot(i):
        return lax.rem(i, SLOTS)

    def own_in(i):
        return remote(
            own.at[lax.rem(i, count)], got.at[1 - inner, slot(i)], ss.at[0, i], rs.at[1 - inner, i], cell, inward
        )

    def own_out(i):
        return remote(own.at[lax.rem(i, count)], got.at[0, slot(i)], ss.at[1, i], rs.at[0, i], cell, outward)

    def relay(i):
        return remote(got.at[1, slot(i)], got.at[2, slot(i)], ss.at[2, i], rs.at[2, i], cell, inward)

    def part(i):
        return remote(got.at[1, slot(i)], got.at[2, slot(i)], ss.at[3, i], rs.at[2, i], cell, outward)

    def cut(q):
        return pl.ds(q * span, span)

    def relay_cut(q):
        return remote(
            got.at[1, final, cut(q)], got.at[2, final, cut(q)], cut_send.at[0, q], cut_recv.at[q], cell, inward
        )

    def part_cut(q):
        return remote(
            got.at[1, final, cut(q)], got.at[2, final, cut(q)], cut_send.at[1, q], cut_recv.at[q], cell, outward
        )

    def arrived(which, i):
        piece = got.at[which, slot(i)]
        remote(piece, piece, ss.at[0, i], rs.at[which, i], cell, inward).wait_recv()

    def face_y(side, i):
        line = own.at[lax.rem(i, count), ny - 1 if side == 0 else 0]
        return remote(line, facey.at[side, i], fys.at[side, i], fyr.at[side, i], y_next if side == 0 else y_last, me)

    def face_x(side, s):
        plane = own.at[count - 1 if side == 0 else 0]
        return remote(plane, facex.at[side, s], fxs.at[side, s], fxr.at[side, s], x_next if side == 0 else x_last, me)

    share = width // blocks

    def lent_rows(c):
        return pl.ds(pl.multiple_of(c * share, share), share)

    def lent_z(k):
        block = (near, far, inward)[k]
        src = coupling.at[lent_rows(cell), pl.ds(pl.multiple_of(block * width, width), width)]
        return remote(src, weights.at[4 + k, lent_rows(cell)], hs.at[k], hr.at[k], cell, inward)

    def lent_peer(q, k):
        piece = weights.at[4 + k, lent_rows(cell)]
        return remote(piece, piece, hs.at[3 + 3 * q + k], hr.at[3 + 3 * q + k], peers[q], me)

    def lent_twin(q, k):
        piece = weights.at[4 + k, lent_rows(cell if q == 3 else peers[q])]
        return remote(piece, piece, hs.at[12 + 3 * q + k], hr.at[12 + 3 * q + k], twin, me)

    def on_faces(i, act):
        act(face_y(0, i))
        act(face_y(1, i))
        pl.when(lax.rem(i, count) == 0)(lambda: act(face_x(1, i // count)))
        pl.when(lax.rem(i, count) == count - 1)(lambda: act(face_x(0, i // count)))

    def start_new(i):
        on_faces(i, lambda copy: copy.start())
        pl.when(is_outer)(lambda: own_in(i).start())

    def wait_sent(i):
        on_faces(i, lambda copy: copy.wait_send())
        own_in(i).wait_send()
        pl.when(jnp.logical_and(is_inner, i < count))(lambda: own_out(i).wait_send())

    def dot(piece, block, lanes):
        return lax.dot_general(
            piece[...].reshape(-1, width),
            weights[block, lanes, :],
            (((1,), (1,)), ((), ())),
            preferred_element_type=jnp.float32,
        )

    def tiles(body):
        @pl.loop(0, width // TILE)
        def _(tile):
            body(pl.ds(pl.multiple_of(tile * TILE, TILE), TILE))

    def free_part(i):
        relay(i).wait_send()
        lag = SLOTS - count
        pl.when(i >= lag)(lambda: part(i - lag).wait_send())

    def give_credit(i):
        @pl.when(i < steps_all - SLOTS)
        def _():
            pl.semaphore_signal(credit, inc=1, device_id=(cell, inward), device_id_type=MESH)

    def early_parts(i):
        pair = pl.ds(i, 2)
        free_part(i)
        free_part(i + 1)

        def tile(lanes):
            value = dot(got.at[0, pair], 4, lanes) + dot(got.at[2, pair], 5, lanes)
            got[1, pair, :, :, lanes] = value.astype(jnp.bfloat16).reshape(2, ny, nz, TILE)

        tiles(tile)
        for each in (i, i + 1):
            part(each).start()
            give_credit(each)

    def late_part(i):
        here = slot(i)
        free_part(i)

        def tile(lanes):
            value = acc[:, lanes] + dot(got.at[2, here], 5, lanes)
            got[1, here, :, :, lanes] = value.astype(jnp.bfloat16).reshape(ny, nz, TILE)

        tiles(tile)
        part(i).start()

    def home_sums(i):
        s, k, here = i // count, lax.rem(i, count), slot(i)

        @pl.when(is_inner)
        def _():
            def both(lanes):
                total[:, lanes] = dot(own.at[k], 0, lanes) + dot(got.at[1, here], 2, lanes)

            tiles(both)

        @pl.when(is_outer)
        def _():
            def one(lanes):
                total[:, lanes] = dot(own.at[k], 0, lanes)

            tiles(one)

        @pl.when(jnp.logical_and(is_inner, s >= 1))
        def _():
            def lent(lanes):
                acc[:, lanes] = dot(own.at[k], 6, lanes)

            tiles(lent)

    def near_sums(i):
        s, here = i // count, slot(i)

        @pl.when(jnp.logical_or(is_inner, s == 0))
        def _():
            arrived(0, i)

            def one(lanes):
                total[:, lanes] = total[:, lanes] - dot(got.at[0, here], 1, lanes)

            tiles(one)

        @pl.when(jnp.logical_and(is_inner, s >= 1))
        def _():
            def lent(lanes):
                acc[:, lanes] = acc[:, lanes] + dot(got.at[0, here], 4, lanes)

            tiles(lent)

    def finish(i):
        s, k, here = i // count, lax.rem(i, count), slot(i)
        arrived(2, i)
        pl.when(jnp.logical_and(is_inner, s >= 1))(lambda: late_part(i))
        wait_sent(i)

        def store(lanes, value):
            new = (total[:, lanes] - value).reshape(ny, nz, TILE)
            dens[k, :, :, lanes] = new
            own[k, :, :, lanes] = new.astype(jnp.bfloat16)

        @pl.when(is_inner)
        def _():
            tiles(lambda lanes: store(lanes, dot(got.at[2, here], 3, lanes)))
            pl.when(s >= 1)(lambda: give_credit(i))

        @pl.when(is_outer)
        def _():
            tiles(lambda lanes: store(lanes, got[2, here, :, :, lanes].reshape(rows, TILE).astype(jnp.float32)))

    def finish_last():
        k = count - 1

        def lines(q):
            return pl.ds(q * span * nz, span * nz)

        @pl.when(is_inner)
        def _():
            part(jnp.int32(last - (SLOTS - count))).wait_send()
            for q in range(CUTS):
                relay_cut(q).wait_send()
                relay_cut(q).wait_recv()

                def piece(lanes):
                    value = acc[lines(q), lanes] + dot(got.at[2, final, cut(q)], 5, lanes)
                    got[1, final, cut(q), :, lanes] = value.astype(jnp.bfloat16).reshape(span, nz, TILE)

                tiles(piece)
                part_cut(q).start()

            def store(lanes):
                value = total[:, lanes] - dot(got.at[2, final], 3, lanes)
                dens[k, :, :, lanes] = value.reshape(ny, nz, TILE)

            tiles(store)

        @pl.when(is_outer)
        def _():
            for q in range(CUTS):
                part_cut(q).wait_recv()

                def store(lanes):
                    value = got[2, final, cut(q), :, lanes].reshape(span * nz, TILE).astype(jnp.float32)
                    dens[k, cut(q), :, lanes] = (total[lines(q), lanes] - value).reshape(span, nz, TILE)

                tiles(store)

        wait_sent(jnp.int32(last))

    def process(i):
        s, k = i // count, lax.rem(i, count)
        home_sums(i)
        face_y(0, i).wait_recv()
        face_y(1, i).wait_recv()

        @pl.when(k == 0)
        def _():
            face_x(0, s).wait_recv()
            old[1, 1 : ny + 1] = facex[0, s].astype(jnp.float32)

        @pl.when(k < count - 1)
        def _():
            above[...] = dens[k + 1]

        @pl.when(k == count - 1)
        def _():
            face_x(1, s).wait_recv()
            above[...] = facex[1, s].astype(jnp.float32)

        spot = lax.broadcasted_iota(jnp.int32, (nz, 512), 0)
        diagonal = lax.broadcasted_iota(jnp.int32, (nz, nz), 0) == lax.broadcasted_iota(jnp.int32, (nz, nz), 1)
        cur = lax.rem(k, 2)
        old[cur, 1 : ny + 1] = dens[k]
        old[cur, 0] = facey[0, i].astype(jnp.float32) * low_ok
        old[cur, ny + 1] = facey[1, i].astype(jnp.float32) * high_ok

        @pl.loop(0, ny)
        def _(y):
            lit = heat[0, k, pl.ds(y, 1), :].astype(jnp.float32)
            warm = jnp.sum(jnp.where(diagonal, lit, 0.0), axis=1, keepdims=True)
            for lane in range(0, width, 512):
                lanes = slice(lane, lane + 512)
                here = old[cur, y + 1, :, lanes]
                new = rates[0:1, lanes] * here
                new += rates[1:2, lanes] * old[1 - cur, y + 1, :, lanes]
                new += rates[2:3, lanes] * above[y, :, lanes]
                new += rates[3:4, lanes] * old[cur, y, :, lanes]
                new += rates[4:5, lanes] * old[cur, y + 2, :, lanes]
                new += rates[5:6, lanes] * jnp.where(spot == 0, 0.0, pltpu.roll(here, 1, 0))
                new += rates[6:7, lanes] * jnp.where(spot == nz - 1, 0.0, pltpu.roll(here, nz - 1, 0))
                line = pl.ds(pl.multiple_of(y * nz, nz), nz)
                total[line, lanes] = new + warm * rates[7:8, lanes] - total[line, lanes]

        near_sums(i)
        pl.when(i < last)(lambda: finish(i))
        pl.when(i == last)(finish_last)
        pl.when(s < STEPS - 1)(lambda: start_new(i + count))

    plane_loads = [pltpu.make_async_copy(phonons.at[0, k], dens.at[k], load_sem.at[4 + k]) for k in range(count)]
    for load in plane_loads:
        load.start()
    order = (me, inward, jnp.clip(outward, 0, 3), far)
    loads = [
        pltpu.make_async_copy(
            coupling.at[:, pl.ds(pl.multiple_of(block * width, width), width)], weights.at[j], load_sem.at[j]
        )
        for j, block in enumerate(order)
    ]
    barrier = pltpu.get_barrier_semaphore()

    def greet(c, m):
        pl.semaphore_signal(barrier, inc=1, device_id=(c, m), device_id_type=MESH)

    greet(cell, inward)
    pl.when(is_inner)(lambda: greet(cell, outward))
    for c in (y_next, y_last, x_next, x_last, twin) + peers:
        greet(c, me)
    for load in loads:
        load.start()
    stay = 1.0 - courant[0:1] - courant[1:2] - courant[2:3] - relaxation[...].reshape(1, width)
    rates[0:1] = stay
    for d in range(3):
        speed = courant[d : d + 1]
        forward = upwind[d : d + 1] == 1
        rates[1 + 2 * d : 2 + 2 * d] = jnp.where(forward, speed, 0.0)
        rates[2 + 2 * d : 3 + 2 * d] = jnp.where(forward, 0.0, speed)
    rates[7:8] = source[...].reshape(1, width)
    pl.semaphore_wait(barrier, 9 + inner)

    for i in range(count):
        plane_loads[i].wait()
        own[i] = dens[i].astype(jnp.bfloat16)
        start_new(jnp.int32(i))

        @pl.when(is_inner)
        def _():
            if i < AHEAD[0]:
                own_in(jnp.int32(i)).start()
            own_out(jnp.int32(i)).start()

        if i in LENT_AFTER:
            pl.when(is_outer)(lambda: lent_z(LENT_AFTER.index(i)).start())

    @pl.loop(0, steps_all + 1)
    def _(t):
        @pl.when(is_inner)
        def _():
            @pl.when(t < steps_all)
            def _():
                arrived(1, t)
                pl.when(t < last)(lambda: relay(t).start())

                @pl.when(t == last)
                def _():
                    for q in range(CUTS):
                        relay_cut(q).start()

            pl.when(t + AHEAD[0] < count)(lambda: own_in(t + AHEAD[0]).start())

            @pl.when(jnp.logical_and(t + AHEAD[1] >= count, t + AHEAD[1] < steps_all))
            def _():
                pl.when(t + AHEAD[1] >= SLOTS)(lambda: pl.semaphore_wait(credit, 1))
                own_in(t + AHEAD[1]).start()

            for k in range(3):

                @pl.when(t == PEER_AT[k])
                def _():
                    lent_z(k).wait_recv()
                    for q in range(3):
                        lent_peer(q, k).start()

                @pl.when(t == TWIN_AT[k])
                def _():
                    for q in range(3):
                        lent_peer(q, k).wait_recv()
                    for q in range(4):
                        lent_twin(q, k).start()

                @pl.when(t == READY_AT[k])
                def _():
                    for q in range(4):
                        lent_twin(q, k).wait_recv()

        @pl.when(t == 1)
        def _():
            for load in loads:
                load.wait()

        @pl.when(t >= 1)
        def _():
            u = t - 1
            process(u)

            @pl.when(jnp.logical_and(is_inner, jnp.logical_and(u >= DRAIN, u < DRAIN + count // 2)))
            def _():
                early_parts(2 * (u - DRAIN))

    @pl.when(is_inner)
    def _():
        for i in range(steps_all - (SLOTS - count), last):
            part(jnp.int32(i)).wait_send()
        for q in range(CUTS):
            part_cut(q).wait_send()
        for k in range(3):
            for q in range(3):
                lent_peer(q, k).wait_send()
            for q in range(4):
                lent_twin(q, k).wait_send()

    @pl.when(is_outer)
    def _():
        for k in range(3):
            lent_z(k).wait_send()


def line_device(phonons, heaters, courant, upwind, relaxation, source, coupling):
    _, count, ny, nz, width = phonons.shape
    calls = STEPS * count
    anywhere, vmem = pl.BlockSpec(memory_space=pl.ANY), pl.BlockSpec(memory_space=pltpu.VMEM)
    dma = pltpu.SemaphoreType.DMA
    half, full = jnp.bfloat16, jnp.float32
    return pl.pallas_call(
        line_kernel,
        out_shape=pltpu.VMEM(phonons.shape, full),
        in_specs=[anywhere, vmem, vmem, vmem, vmem, vmem, anywhere],
        out_specs=vmem,
        scratch_shapes=[
            pltpu.VMEM((ny, nz, width), full),
            pltpu.VMEM((count, ny, nz, width), half),
            pltpu.VMEM((3, SLOTS, ny, nz, width), half),
            pltpu.VMEM((7, width, width), half),
            pltpu.VMEM((2, ny + 2, nz, width), full),
            pltpu.VMEM((2, STEPS, ny, nz, width), half),
            pltpu.VMEM((2, calls, nz, width), half),
            pltpu.VMEM((ny * nz, width), full),
            pltpu.VMEM((ny * nz, width), full),
            pltpu.VMEM((8, width), full),
            dma((4 + count,)),
            dma((4, calls)),
            dma((3, calls)),
            dma((2, calls)),
            dma((2, calls)),
            dma((2, STEPS)),
            dma((2, STEPS)),
            dma((24,)),
            dma((24,)),
            dma((2, CUTS)),
            dma((CUTS,)),
            pltpu.SemaphoreType.REGULAR,
        ],
        compiler_params=pltpu.CompilerParams(
            collective_id=0, has_side_effects=True, vmem_limit_bytes=64 * 2**20 - 2**18 - 4 * phonons.size
        ),
    )(phonons, heaters, courant, upwind, relaxation, source, coupling)


def shifted(block, axis, distance):
    devices = range(lax.axis_size(axis))
    route = [((i - distance) % len(devices), i) for i in devices]
    return lax.ppermute(block, axis, route)


def upstream(density, forward, axis):
    widths = [(0, 0)] * density.ndim
    widths[axis] = (1, 1)
    padded = jnp.pad(density, widths)
    length_axis = density.shape[axis]
    behind = lax.slice_in_dim(padded, 0, length_axis, axis=axis)
    ahead = lax.slice_in_dim(padded, 2, length_axis + 2, axis=axis)
    return jnp.where(forward, behind, ahead)


def scatter_term(rounded, coupling):
    contract = (((1,), (1,)), ((), ()))
    gathered = lax.all_gather(rounded, "modes", axis=1, tiled=True)
    return lax.dot_general(gathered, coupling, contract, preferred_element_type=jnp.float32)


def advect(density, courant, upwind, masks):
    lower_y_ok, upper_y_ok = masks
    forward_x = upwind[0] == 1
    forward_y = upwind[1] == 1
    forward_z = upwind[2] == 1
    below_x = shifted(density[-1].astype(jnp.bfloat16), "cells", GY).astype(jnp.float32)
    above_x = shifted(density[0], "cells", -GY)
    below_y = (
        shifted(density[:, -1].astype(jnp.bfloat16), "cells", 1).astype(jnp.float32) * lower_y_ok
    )
    above_y = (
        shifted(density[:, 0].astype(jnp.bfloat16), "cells", -1).astype(jnp.float32) * upper_y_ok
    )
    upstream_z = upstream(density, forward_z, 2)
    transport = courant[0] * (density - upstream(density, forward_x, 0))
    transport = transport + courant[1] * (density - upstream(density, forward_y, 1))
    transport = transport + courant[2] * (density - upstream_z)
    transport = transport.at[0].add(-courant[0] * jnp.where(forward_x, below_x, 0.0))
    transport = transport.at[-1].add(-courant[0] * jnp.where(forward_x, 0.0, above_x))
    transport = transport.at[:, 0].add(-courant[1] * jnp.where(forward_y, below_y, 0.0))
    transport = transport.at[:, -1].add(-courant[1] * jnp.where(forward_y, 0.0, above_y))
    return transport


def per_device(phonons, heaters, courant, upwind, relaxation, source, coupling):
    density = phonons[0]
    cell_count = density.shape[0] * density.shape[1] * density.shape[2]
    mode_count = density.shape[3]
    block_total = lax.axis_size("cells")
    position = (lax.axis_index("cells") + 2) % block_total
    column = position % GY
    masks = ((column != 0).astype(jnp.float32), (column != GY - 1).astype(jnp.float32))
    heating = heaters[0].astype(jnp.float32)[..., None] * source
    for repeat in range(STEPS):
        rounded = density.astype(jnp.bfloat16).reshape(cell_count, mode_count)
        scattered = scatter_term(rounded, coupling).reshape(density.shape)
        transport = advect(density, courant, upwind, masks)
        density = density - transport - relaxation * density - scattered + heating
    return density[None]


def solution(mesh):
    placed = (
        P("cells", None, None, None, "modes"),
        P("cells", None, None, None),
        P(None, "modes"),
        P(None, "modes"),
        P("modes"),
        P("modes"),
        P("modes", None),
    )
    on_line = mesh.shape["modes"] == 4 and mesh.shape["cells"] == 8
    return jax.shard_map(
        line_device if on_line else per_device,
        mesh=mesh,
        in_specs=placed,
        out_specs=P("cells", None, None, None, "modes"),
        check_vma=False,
    )
```

```python
import jax
import jax.numpy as jnp
from jax import lax
from jax.experimental import pallas as pl
from jax.experimental.pallas import tpu as pltpu
from jax.sharding import PartitionSpec as P

GY = 4
STEPS = 2

TILE = 768
SLOTS = 12
AHEAD = (3, 1)
PEER_AT = (1, 2, 4)
TWIN_AT = (3, 4, 6)
READY_AT = (5, 5, 8)
LENT_AFTER = (1, 2, 4)
DRAIN = 4
CUTS = 2
MESH = pl.DeviceIdType.MESH


def line_kernel(phonons, heaters, courants, upwinds, relaxations, sources, coupling, out, above, own, got, weights, old,
                facex, facey, total, acc, rates, heat, courant, upwind, relaxation,
                source, load_sem, ss, rs, fys, fyr, fxs, fxr, hs, hr, cut_send, cut_recv, credit):
    cell, me = lax.axis_index("cells"), lax.axis_index("modes")
    count, ny, nz, width = own.shape
    dens = out.at[0]
    steps_all = STEPS * count
    last, final = steps_all - 1, (steps_all - 1) % SLOTS
    span = ny // CUTS
    rows = ny * nz
    blocks = lax.axis_size("cells")
    half = me // 2
    inner = lax.rem((me + 1) // 2, 2)
    is_inner = inner == 1
    is_outer = inner == 0
    toward = 1 - 2 * half
    inward, outward = me + toward, me - toward
    near, far = me + 2 * toward, 3 - 3 * half
    y_next, y_last = lax.rem(cell + 1, blocks), lax.rem(cell + blocks - 1, blocks)
    x_next, x_last = lax.rem(cell + GY, blocks), lax.rem(cell + blocks - GY, blocks)
    twin = cell + 1 - 2 * lax.rem(cell, 2)
    flip2 = 2 - 4 * lax.rem(cell // 2, 2)
    flip4 = 4 - 8 * lax.rem(cell // 4, 2)
    peers = (cell + flip2, cell + flip4, cell + flip2 + flip4)
    column = lax.rem(lax.rem(cell + 2, blocks), GY)
    low_ok = jnp.where(column != 0, 1.0, 0.0).astype(jnp.float32)
    high_ok = jnp.where(column != GY - 1, 1.0, 0.0).astype(jnp.float32)

    def remote(src, dst, send, recv, c, m):
        return pltpu.make_async_remote_copy(
            src_ref=src, dst_ref=dst, send_sem=send, recv_sem=recv, device_id=(c, m), device_id_type=MESH
        )

    def slot(i):
        return lax.rem(i, SLOTS)

    def own_in(i):
        return remote(
            own.at[lax.rem(i, count)], got.at[1 - inner, slot(i)], ss.at[0, i], rs.at[1 - inner, i], cell, inward
        )

    def own_out(i):
        return remote(own.at[lax.rem(i, count)], got.at[0, slot(i)], ss.at[1, i], rs.at[0, i], cell, outward)

    def relay(i):
        return remote(got.at[1, slot(i)], got.at[2, slot(i)], ss.at[2, i], rs.at[2, i], cell, inward)

    def part(i):
        return remote(got.at[1, slot(i)], got.at[2, slot(i)], ss.at[3, i], rs.at[2, i], cell, outward)

    def cut(q):
        return pl.ds(q * span, span)

    def relay_cut(q):
        return remote(
            got.at[1, final, cut(q)], got.at[2, final, cut(q)], cut_send.at[0, q], cut_recv.at[q], cell, inward
        )

    def part_cut(q):
        return remote(
            got.at[1, final, cut(q)], got.at[2, final, cut(q)], cut_send.at[1, q], cut_recv.at[q], cell, outward
        )

    def arrived(which, i):
        piece = got.at[which, slot(i)]
        remote(piece, piece, ss.at[0, i], rs.at[which, i], cell, inward).wait_recv()

    def face_y(side, i):
        line = own.at[lax.rem(i, count), ny - 1 if side == 0 else 0]
        return remote(line, facey.at[side, i], fys.at[side, i], fyr.at[side, i], y_next if side == 0 else y_last, me)

    def face_x(side, s):
        plane = own.at[count - 1 if side == 0 else 0]
        return remote(plane, facex.at[side, s], fxs.at[side, s], fxr.at[side, s], x_next if side == 0 else x_last, me)

    share = width // blocks

    def lent_rows(c):
        return pl.ds(pl.multiple_of(c * share, share), share)

    def lent_z(k):
        block = (near, far, inward)[k]
        src = coupling.at[lent_rows(cell), pl.ds(pl.multiple_of(block * width, width), width)]
        return remote(src, weights.at[4 + k, lent_rows(cell)], hs.at[k], hr.at[k], cell, inward)

    def lent_peer(q, k):
        piece = weights.at[4 + k, lent_rows(cell)]
        return remote(piece, piece, hs.at[3 + 3 * q + k], hr.at[3 + 3 * q + k], peers[q], me)

    def lent_twin(q, k):
        piece = weights.at[4 + k, lent_rows(cell if q == 3 else peers[q])]
        return remote(piece, piece, hs.at[12 + 3 * q + k], hr.at[12 + 3 * q + k], twin, me)

    def on_faces(i, act):
        act(face_y(0, i))
        act(face_y(1, i))
        pl.when(lax.rem(i, count) == 0)(lambda: act(face_x(1, i // count)))
        pl.when(lax.rem(i, count) == count - 1)(lambda: act(face_x(0, i // count)))

    def start_new(i):
        pl.when(is_outer)(lambda: own_in(i).start())
        on_faces(i, lambda copy: copy.start())

    def wait_sent(i):
        on_faces(i, lambda copy: copy.wait_send())
        own_in(i).wait_send()
        pl.when(jnp.logical_and(is_inner, i < count))(lambda: own_out(i).wait_send())

    def dot(piece, block, lanes):
        return lax.dot_general(
            piece[...].reshape(-1, width),
            weights[block, lanes, :],
            (((1,), (1,)), ((), ())),
            preferred_element_type=jnp.float32,
        )

    def tiles(body):
        @pl.loop(0, width // TILE)
        def _(tile):
            body(pl.ds(pl.multiple_of(tile * TILE, TILE), TILE))

    def free_part(i):
        relay(i).wait_send()
        lag = SLOTS - count
        pl.when(i >= lag)(lambda: part(i - lag).wait_send())

    def give_credit(i):
        @pl.when(i < steps_all - SLOTS)
        def _():
            pl.semaphore_signal(credit, inc=1, device_id=(cell, inward), device_id_type=MESH)

    def early_parts(i):
        pair = pl.ds(i, 2)
        free_part(i)
        free_part(i + 1)

        def tile(lanes):
            value = dot(got.at[0, pair], 4, lanes) + dot(got.at[2, pair], 5, lanes)
            got[1, pair, :, :, lanes] = value.astype(jnp.bfloat16).reshape(2, ny, nz, TILE)

        tiles(tile)
        for each in (i, i + 1):
            part(each).start()
            give_credit(each)

    def late_part(i):
        here, bank = slot(i), i // last
        free_part(i)

        def tile(lanes):
            value = acc[bank, :, lanes] + dot(got.at[2, here], 5, lanes)
            got[1, here, :, :, lanes] = value.astype(jnp.bfloat16).reshape(ny, nz, TILE)

        tiles(tile)
        part(i).start()

    def home_sums(i):
        bank = i // last
        s, k, here = i // count, lax.rem(i, count), slot(i)

        @pl.when(is_inner)
        def _():
            def both(lanes):
                total[bank, :, lanes] = dot(own.at[k], 0, lanes) + dot(got.at[1, here], 2, lanes)

            tiles(both)

        @pl.when(is_outer)
        def _():
            def one(lanes):
                total[bank, :, lanes] = dot(own.at[k], 0, lanes)

            tiles(one)

        @pl.when(jnp.logical_and(is_inner, s >= 1))
        def _():
            def lent(lanes):
                acc[bank, :, lanes] = dot(own.at[k], 6, lanes)

            tiles(lent)

    def near_sums(i):
        s, here, bank = i // count, slot(i), i // last

        @pl.when(jnp.logical_or(is_inner, s == 0))
        def _():
            arrived(0, i)

            def one(lanes):
                total[bank, :, lanes] = total[bank, :, lanes] - dot(got.at[0, here], 1, lanes)

            tiles(one)

        @pl.when(jnp.logical_and(is_inner, s >= 1))
        def _():
            def lent(lanes):
                acc[bank, :, lanes] = acc[bank, :, lanes] + dot(got.at[0, here], 4, lanes)

            tiles(lent)

    def finish(i):
        bank = i // last
        s, k, here = i // count, lax.rem(i, count), slot(i)
        arrived(2, i)
        pl.when(jnp.logical_and(is_inner, s >= 1))(lambda: late_part(i))
        wait_sent(i)

        def store(lanes, value):
            new = (total[bank, :, lanes] - value).reshape(ny, nz, TILE)
            dens[k, :, :, lanes] = new
            own[k, :, :, lanes] = new.astype(jnp.bfloat16)

        @pl.when(is_inner)
        def _():
            tiles(lambda lanes: store(lanes, dot(got.at[2, here], 3, lanes)))
            pl.when(s >= 1)(lambda: give_credit(i))

        @pl.when(is_outer)
        def _():
            tiles(lambda lanes: store(lanes, got[2, here, :, :, lanes].reshape(rows, TILE).astype(jnp.float32)))

    def finish_last():
        k, bank = count - 1, 1

        def lines(q):
            return pl.ds(q * span * nz, span * nz)

        @pl.when(is_inner)
        def _():
            part(jnp.int32(last - (SLOTS - count))).wait_send()
            for q in range(CUTS):
                relay_cut(q).wait_send()
                relay_cut(q).wait_recv()

                def piece(lanes):
                    value = acc[bank, lines(q), lanes] + dot(got.at[2, final, cut(q)], 5, lanes)
                    got[1, final, cut(q), :, lanes] = value.astype(jnp.bfloat16).reshape(span, nz, TILE)

                tiles(piece)
                part_cut(q).start()

            def store(lanes):
                value = total[bank, :, lanes] - dot(got.at[2, final], 3, lanes)
                dens[k, :, :, lanes] = value.reshape(ny, nz, TILE)

            tiles(store)

        @pl.when(is_outer)
        def _():
            for q in range(CUTS):
                part_cut(q).wait_recv()

                def store(lanes):
                    value = got[2, final, cut(q), :, lanes].reshape(span * nz, TILE).astype(jnp.float32)
                    dens[k, cut(q), :, lanes] = (total[bank, lines(q), lanes] - value).reshape(span, nz, TILE)

                tiles(store)

        wait_sent(jnp.int32(last))

    def prepare(i):
        bank = i // last
        s, k = i // count, lax.rem(i, count)
        home_sums(i)
        face_y(0, i).wait_recv()
        face_y(1, i).wait_recv()

        @pl.when(k == 0)
        def _():
            face_x(0, s).wait_recv()
            old[1, 1 : ny + 1] = facex[0, s].astype(jnp.float32)

        @pl.when(k < count - 1)
        def _():
            above[...] = dens[k + 1]

        @pl.when(k == count - 1)
        def _():
            face_x(1, s).wait_recv()
            above[...] = facex[1, s].astype(jnp.float32)

        spot = lax.broadcasted_iota(jnp.int32, (nz, 512), 0)
        diagonal = lax.broadcasted_iota(jnp.int32, (nz, nz), 0) == lax.broadcasted_iota(jnp.int32, (nz, nz), 1)
        cur = lax.rem(k, 2)
        old[cur, 1 : ny + 1] = dens[k]
        old[cur, 0] = facey[0, i].astype(jnp.float32) * low_ok
        old[cur, ny + 1] = facey[1, i].astype(jnp.float32) * high_ok

        @pl.loop(0, ny)
        def _(y):
            lit = heat[0, k, pl.ds(y, 1), :].astype(jnp.float32)
            warm = jnp.sum(jnp.where(diagonal, lit, 0.0), axis=1, keepdims=True)
            for lane in range(0, width, 512):
                lanes = slice(lane, lane + 512)
                here = old[cur, y + 1, :, lanes]
                new = rates[0:1, lanes] * here
                new += rates[1:2, lanes] * old[1 - cur, y + 1, :, lanes]
                new += rates[2:3, lanes] * above[y, :, lanes]
                new += rates[3:4, lanes] * old[cur, y, :, lanes]
                new += rates[4:5, lanes] * old[cur, y + 2, :, lanes]
                new += rates[5:6, lanes] * jnp.where(spot == 0, 0.0, pltpu.roll(here, 1, 0))
                new += rates[6:7, lanes] * jnp.where(spot == nz - 1, 0.0, pltpu.roll(here, nz - 1, 0))
                line = pl.ds(pl.multiple_of(y * nz, nz), nz)
                total[bank, line, lanes] = new + warm * rates[7:8, lanes] - total[bank, line, lanes]

    def process(i):
        s, k = i // count, lax.rem(i, count)
        pl.when(i < last)(lambda: prepare(i))
        near_sums(i)
        pl.when(i == last - 1)(lambda: prepare(jnp.int32(last)))
        pl.when(i < last)(lambda: finish(i))
        pl.when(i == last)(finish_last)
        pl.when(s < STEPS - 1)(lambda: start_new(i + count))

    plane_loads = [pltpu.make_async_copy(phonons.at[0, k], dens.at[k], load_sem.at[4 + k]) for k in range(count)]
    for load in plane_loads:
        load.start()
    order = (me, inward, jnp.clip(outward, 0, 3), far)
    loads = [
        pltpu.make_async_copy(
            coupling.at[:, pl.ds(pl.multiple_of(block * width, width), width)], weights.at[j], load_sem.at[j]
        )
        for j, block in enumerate(order)
    ]
    barrier = pltpu.get_barrier_semaphore()

    def greet(c, m):
        pl.semaphore_signal(barrier, inc=1, device_id=(c, m), device_id_type=MESH)

    greet(cell, inward)
    pl.when(is_inner)(lambda: greet(cell, outward))
    for c in (y_next, y_last, x_next, x_last, twin) + peers:
        greet(c, me)
    small = ((heaters, heat), (courants, courant), (upwinds, upwind), (relaxations, relaxation), (sources, source))
    small_loads = [
        pltpu.make_async_copy(far_ref, near_ref, load_sem.at[4 + count + j]) for j, (far_ref, near_ref) in enumerate(small)
    ]
    for load in loads + small_loads:
        load.start()

    def make_rates():
        for load in small_loads:
            load.wait()
        stay = 1.0 - courant[0:1] - courant[1:2] - courant[2:3] - relaxation[...].reshape(1, width)
        rates[0:1] = stay
        for d in range(3):
            speed = courant[d : d + 1]
            forward = upwind[d : d + 1] == 1
            rates[1 + 2 * d : 2 + 2 * d] = jnp.where(forward, speed, 0.0)
            rates[2 + 2 * d : 3 + 2 * d] = jnp.where(forward, 0.0, speed)
        rates[7:8] = source[...].reshape(1, width)

    pl.semaphore_wait(barrier, 9 + inner)

    for i in range(count):
        plane_loads[i].wait()
        own[i] = dens[i].astype(jnp.bfloat16)

        @pl.when(is_inner)
        def _():
            if i < AHEAD[0]:
                own_in(jnp.int32(i)).start()
            own_out(jnp.int32(i)).start()

        start_new(jnp.int32(i))

        if i in LENT_AFTER:
            pl.when(is_outer)(lambda: lent_z(LENT_AFTER.index(i)).start())

    @pl.loop(0, steps_all + 1)
    def _(t):
        @pl.when(is_inner)
        def _():
            @pl.when(t < steps_all)
            def _():
                arrived(1, t)
                pl.when(t < last)(lambda: relay(t).start())

                @pl.when(t == last)
                def _():
                    for q in range(CUTS):
                        relay_cut(q).start()

            pl.when(t + AHEAD[0] < count)(lambda: own_in(t + AHEAD[0]).start())

            @pl.when(jnp.logical_and(t + AHEAD[1] >= count, t + AHEAD[1] < steps_all))
            def _():
                pl.when(t + AHEAD[1] >= SLOTS)(lambda: pl.semaphore_wait(credit, 1))
                own_in(t + AHEAD[1]).start()

            for k in range(3):

                @pl.when(t == PEER_AT[k])
                def _():
                    lent_z(k).wait_recv()
                    for q in range(3):
                        lent_peer(q, k).start()

                @pl.when(t == TWIN_AT[k])
                def _():
                    for q in range(3):
                        lent_peer(q, k).wait_recv()
                    for q in range(4):
                        lent_twin(q, k).start()

                @pl.when(t == READY_AT[k])
                def _():
                    for q in range(4):
                        lent_twin(q, k).wait_recv()

        @pl.when(t == 1)
        def _():
            for load in loads:
                load.wait()
            make_rates()

        @pl.when(t >= 1)
        def _():
            u = t - 1
            process(u)

            @pl.when(jnp.logical_and(is_inner, jnp.logical_and(u >= DRAIN, u < DRAIN + count // 2)))
            def _():
                early_parts(2 * (u - DRAIN))

    @pl.when(is_inner)
    def _():
        for i in range(steps_all - (SLOTS - count), last):
            part(jnp.int32(i)).wait_send()
        for q in range(CUTS):
            part_cut(q).wait_send()
        for k in range(3):
            for q in range(3):
                lent_peer(q, k).wait_send()
            for q in range(4):
                lent_twin(q, k).wait_send()

    @pl.when(is_outer)
    def _():
        for k in range(3):
            lent_z(k).wait_send()


def line_device(phonons, heaters, courant, upwind, relaxation, source, coupling):
    _, count, ny, nz, width = phonons.shape
    calls = STEPS * count
    anywhere, vmem = pl.BlockSpec(memory_space=pl.ANY), pl.BlockSpec(memory_space=pltpu.VMEM)
    dma = pltpu.SemaphoreType.DMA
    half, full = jnp.bfloat16, jnp.float32
    return pl.pallas_call(
        line_kernel,
        out_shape=pltpu.VMEM(phonons.shape, full),
        in_specs=[anywhere] * 7,
        out_specs=vmem,
        scratch_shapes=[
            pltpu.VMEM((ny, nz, width), full),
            pltpu.VMEM((count, ny, nz, width), half),
            pltpu.VMEM((3, SLOTS, ny, nz, width), half),
            pltpu.VMEM((7, width, width), half),
            pltpu.VMEM((2, ny + 2, nz, width), full),
            pltpu.VMEM((2, STEPS, ny, nz, width), half),
            pltpu.VMEM((2, calls, nz, width), half),
            pltpu.VMEM((2, ny * nz, width), full),
            pltpu.VMEM((2, ny * nz, width), full),
            pltpu.VMEM((8, width), full),
            pltpu.VMEM(heaters.shape, heaters.dtype),
            pltpu.VMEM(courant.shape, full),
            pltpu.VMEM(upwind.shape, upwind.dtype),
            pltpu.VMEM(relaxation.shape, full),
            pltpu.VMEM(source.shape, full),
            dma((9 + count,)),
            dma((4, calls)),
            dma((3, calls)),
            dma((2, calls)),
            dma((2, calls)),
            dma((2, STEPS)),
            dma((2, STEPS)),
            dma((24,)),
            dma((24,)),
            dma((2, CUTS)),
            dma((CUTS,)),
            pltpu.SemaphoreType.REGULAR,
        ],
        compiler_params=pltpu.CompilerParams(
            collective_id=0, has_side_effects=True, vmem_limit_bytes=64 * 2**20 - 2**18 - 4 * phonons.size
        ),
    )(phonons, heaters, courant, upwind, relaxation, source, coupling)


def shifted(block, axis, distance):
    devices = range(lax.axis_size(axis))
    route = [((i - distance) % len(devices), i) for i in devices]
    return lax.ppermute(block, axis, route)


def upstream(density, forward, axis):
    widths = [(0, 0)] * density.ndim
    widths[axis] = (1, 1)
    padded = jnp.pad(density, widths)
    length_axis = density.shape[axis]
    behind = lax.slice_in_dim(padded, 0, length_axis, axis=axis)
    ahead = lax.slice_in_dim(padded, 2, length_axis + 2, axis=axis)
    return jnp.where(forward, behind, ahead)


def scatter_term(rounded, coupling):
    contract = (((1,), (1,)), ((), ()))
    gathered = lax.all_gather(rounded, "modes", axis=1, tiled=True)
    return lax.dot_general(gathered, coupling, contract, preferred_element_type=jnp.float32)


def advect(density, courant, upwind, masks):
    lower_y_ok, upper_y_ok = masks
    forward_x = upwind[0] == 1
    forward_y = upwind[1] == 1
    forward_z = upwind[2] == 1
    below_x = shifted(density[-1].astype(jnp.bfloat16), "cells", GY).astype(jnp.float32)
    above_x = shifted(density[0], "cells", -GY)
    below_y = (
        shifted(density[:, -1].astype(jnp.bfloat16), "cells", 1).astype(jnp.float32) * lower_y_ok
    )
    above_y = (
        shifted(density[:, 0].astype(jnp.bfloat16), "cells", -1).astype(jnp.float32) * upper_y_ok
    )
    upstream_z = upstream(density, forward_z, 2)
    transport = courant[0] * (density - upstream(density, forward_x, 0))
    transport = transport + courant[1] * (density - upstream(density, forward_y, 1))
    transport = transport + courant[2] * (density - upstream_z)
    transport = transport.at[0].add(-courant[0] * jnp.where(forward_x, below_x, 0.0))
    transport = transport.at[-1].add(-courant[0] * jnp.where(forward_x, 0.0, above_x))
    transport = transport.at[:, 0].add(-courant[1] * jnp.where(forward_y, below_y, 0.0))
    transport = transport.at[:, -1].add(-courant[1] * jnp.where(forward_y, 0.0, above_y))
    return transport


def per_device(phonons, heaters, courant, upwind, relaxation, source, coupling):
    density = phonons[0]
    cell_count = density.shape[0] * density.shape[1] * density.shape[2]
    mode_count = density.shape[3]
    block_total = lax.axis_size("cells")
    position = (lax.axis_index("cells") + 2) % block_total
    column = position % GY
    masks = ((column != 0).astype(jnp.float32), (column != GY - 1).astype(jnp.float32))
    heating = heaters[0].astype(jnp.float32)[..., None] * source
    for repeat in range(STEPS):
        rounded = density.astype(jnp.bfloat16).reshape(cell_count, mode_count)
        scattered = scatter_term(rounded, coupling).reshape(density.shape)
        transport = advect(density, courant, upwind, masks)
        density = density - transport - relaxation * density - scattered + heating
    return density[None]


def solution(mesh):
    placed = (
        P("cells", None, None, None, "modes"),
        P("cells", None, None, None),
        P(None, "modes"),
        P(None, "modes"),
        P("modes"),
        P("modes"),
        P("modes", None),
    )
    on_line = mesh.shape["modes"] == 4 and mesh.shape["cells"] == 8
    return jax.shard_map(
        line_device if on_line else per_device,
        mesh=mesh,
        in_specs=placed,
        out_specs=P("cells", None, None, None, "modes"),
        check_vma=False,
    )
```

```python
import jax
import jax.numpy as jnp
from jax import lax
from jax.experimental import pallas as pl
from jax.experimental.pallas import tpu as pltpu
from jax.sharding import PartitionSpec as P

GY = 4
STEPS = 2

TILE = 768
SLOTS = 12
AHEAD = (3, 1)
PEER_AT = (1, 2, 4)
TWIN_AT = (3, 4, 6)
READY_AT = (5, 5, 8)
LENT_AFTER = (1, 2, 4)
DRAIN = 4
CUTS = 3
MESH = pl.DeviceIdType.MESH


def line_kernel(phonons, heaters, courants, upwinds, relaxations, sources, coupling, out, above, own, got, weights, old,
                facex, facey, total, acc, rates, heat, courant, upwind, relaxation,
                source, load_sem, ss, rs, fys, fyr, fxs, fxr, hs, hr, cut_send, cut_recv, credit):
    cell, me = lax.axis_index("cells"), lax.axis_index("modes")
    count, ny, nz, width = own.shape
    dens = out.at[0]
    steps_all = STEPS * count
    last, final = steps_all - 1, (steps_all - 1) % SLOTS
    edges = [ny - (CUTS - q) * ny // CUTS for q in range(CUTS + 1)]
    rows = ny * nz
    blocks = lax.axis_size("cells")
    half = me // 2
    inner = lax.rem((me + 1) // 2, 2)
    is_inner = inner == 1
    is_outer = inner == 0
    toward = 1 - 2 * half
    inward, outward = me + toward, me - toward
    near, far = me + 2 * toward, 3 - 3 * half
    y_next, y_last = lax.rem(cell + 1, blocks), lax.rem(cell + blocks - 1, blocks)
    x_next, x_last = lax.rem(cell + GY, blocks), lax.rem(cell + blocks - GY, blocks)
    twin = cell + 1 - 2 * lax.rem(cell, 2)
    flip2 = 2 - 4 * lax.rem(cell // 2, 2)
    flip4 = 4 - 8 * lax.rem(cell // 4, 2)
    peers = (cell + flip2, cell + flip4, cell + flip2 + flip4)
    column = lax.rem(lax.rem(cell + 2, blocks), GY)
    low_ok = jnp.where(column != 0, 1.0, 0.0).astype(jnp.float32)
    high_ok = jnp.where(column != GY - 1, 1.0, 0.0).astype(jnp.float32)

    def remote(src, dst, send, recv, c, m):
        return pltpu.make_async_remote_copy(
            src_ref=src, dst_ref=dst, send_sem=send, recv_sem=recv, device_id=(c, m), device_id_type=MESH
        )

    def slot(i):
        return lax.rem(i, SLOTS)

    def own_in(i):
        return remote(
            own.at[lax.rem(i, count)], got.at[1 - inner, slot(i)], ss.at[0, i], rs.at[1 - inner, i], cell, inward
        )

    def own_out(i):
        return remote(own.at[lax.rem(i, count)], got.at[0, slot(i)], ss.at[1, i], rs.at[0, i], cell, outward)

    def relay(i):
        return remote(got.at[1, slot(i)], got.at[2, slot(i)], ss.at[2, i], rs.at[2, i], cell, inward)

    def part(i):
        return remote(got.at[1, slot(i)], got.at[2, slot(i)], ss.at[3, i], rs.at[2, i], cell, outward)

    def cut(q):
        return pl.ds(edges[q], edges[q + 1] - edges[q])

    def relay_cut(q):
        return remote(
            got.at[1, final, cut(q)], got.at[2, final, cut(q)], cut_send.at[0, q], cut_recv.at[q], cell, inward
        )

    def part_cut(q):
        return remote(
            got.at[1, final, cut(q)], got.at[2, final, cut(q)], cut_send.at[1, q], cut_recv.at[q], cell, outward
        )

    def arrived(which, i):
        piece = got.at[which, slot(i)]
        remote(piece, piece, ss.at[0, i], rs.at[which, i], cell, inward).wait_recv()

    def face_y(side, i):
        line = own.at[lax.rem(i, count), ny - 1 if side == 0 else 0]
        return remote(line, facey.at[side, i], fys.at[side, i], fyr.at[side, i], y_next if side == 0 else y_last, me)

    def face_x(side, s):
        plane = own.at[count - 1 if side == 0 else 0]
        return remote(plane, facex.at[side, s], fxs.at[side, s], fxr.at[side, s], x_next if side == 0 else x_last, me)

    share = width // blocks

    def lent_rows(c):
        return pl.ds(pl.multiple_of(c * share, share), share)

    def lent_z(k):
        block = (near, far, inward)[k]
        src = coupling.at[lent_rows(cell), pl.ds(pl.multiple_of(block * width, width), width)]
        return remote(src, weights.at[4 + k, lent_rows(cell)], hs.at[k], hr.at[k], cell, inward)

    def lent_peer(q, k):
        piece = weights.at[4 + k, lent_rows(cell)]
        return remote(piece, piece, hs.at[3 + 3 * q + k], hr.at[3 + 3 * q + k], peers[q], me)

    def lent_twin(q, k):
        piece = weights.at[4 + k, lent_rows(cell if q == 3 else peers[q])]
        return remote(piece, piece, hs.at[12 + 3 * q + k], hr.at[12 + 3 * q + k], twin, me)

    def on_faces(i, act):
        act(face_y(0, i))
        act(face_y(1, i))
        pl.when(lax.rem(i, count) == 0)(lambda: act(face_x(1, i // count)))
        pl.when(lax.rem(i, count) == count - 1)(lambda: act(face_x(0, i // count)))

    def start_new(i):
        pl.when(is_outer)(lambda: own_in(i).start())
        on_faces(i, lambda copy: copy.start())

    def wait_sent(i):
        on_faces(i, lambda copy: copy.wait_send())
        own_in(i).wait_send()
        pl.when(jnp.logical_and(is_inner, i < count))(lambda: own_out(i).wait_send())

    def dot(piece, block, lanes):
        return lax.dot_general(
            piece[...].reshape(-1, width),
            weights[block, lanes, :],
            (((1,), (1,)), ((), ())),
            preferred_element_type=jnp.float32,
        )

    def tiles(body):
        @pl.loop(0, width // TILE)
        def _(tile):
            body(pl.ds(pl.multiple_of(tile * TILE, TILE), TILE))

    def free_part(i):
        relay(i).wait_send()
        lag = SLOTS - count
        pl.when(i >= lag)(lambda: part(i - lag).wait_send())

    def give_credit(i):
        @pl.when(i < steps_all - SLOTS)
        def _():
            pl.semaphore_signal(credit, inc=1, device_id=(cell, inward), device_id_type=MESH)

    def early_parts(i):
        pair = pl.ds(i, 2)
        free_part(i)
        free_part(i + 1)

        def tile(lanes):
            value = dot(got.at[0, pair], 4, lanes) + dot(got.at[2, pair], 5, lanes)
            got[1, pair, :, :, lanes] = value.astype(jnp.bfloat16).reshape(2, ny, nz, TILE)

        tiles(tile)
        for each in (i, i + 1):
            part(each).start()
            give_credit(each)

    def late_part(i):
        here, bank = slot(i), lax.rem(i, 2)
        free_part(i)

        def tile(lanes):
            value = acc[bank, :, lanes] + dot(got.at[2, here], 5, lanes)
            got[1, here, :, :, lanes] = value.astype(jnp.bfloat16).reshape(ny, nz, TILE)

        tiles(tile)
        part(i).start()

    def home_sums(i):
        bank = lax.rem(i, 2)
        s, k, here = i // count, lax.rem(i, count), slot(i)

        @pl.when(is_inner)
        def _():
            def both(lanes):
                total[bank, :, lanes] = dot(own.at[k], 0, lanes) + dot(got.at[1, here], 2, lanes)

            tiles(both)

        @pl.when(is_outer)
        def _():
            def one(lanes):
                total[bank, :, lanes] = dot(own.at[k], 0, lanes)

            tiles(one)

        @pl.when(jnp.logical_and(is_inner, s >= 1))
        def _():
            def lent(lanes):
                acc[bank, :, lanes] = dot(own.at[k], 6, lanes)

            tiles(lent)

    def near_sums(i):
        s, here, bank = i // count, slot(i), lax.rem(i, 2)

        @pl.when(jnp.logical_or(is_inner, s == 0))
        def _():
            arrived(0, i)

            def one(lanes):
                total[bank, :, lanes] = total[bank, :, lanes] - dot(got.at[0, here], 1, lanes)

            tiles(one)

        @pl.when(jnp.logical_and(is_inner, s >= 1))
        def _():
            def lent(lanes):
                acc[bank, :, lanes] = acc[bank, :, lanes] + dot(got.at[0, here], 4, lanes)

            tiles(lent)

    def finish(i):
        bank = lax.rem(i, 2)
        s, k, here = i // count, lax.rem(i, count), slot(i)
        arrived(2, i)
        pl.when(jnp.logical_and(is_inner, s >= 1))(lambda: late_part(i))
        wait_sent(i)

        def store(lanes, value):
            new = (total[bank, :, lanes] - value).reshape(ny, nz, TILE)
            dens[k, :, :, lanes] = new
            own[k, :, :, lanes] = new.astype(jnp.bfloat16)

        @pl.when(is_inner)
        def _():
            tiles(lambda lanes: store(lanes, dot(got.at[2, here], 3, lanes)))
            pl.when(s >= 1)(lambda: give_credit(i))

        @pl.when(is_outer)
        def _():
            tiles(lambda lanes: store(lanes, got[2, here, :, :, lanes].reshape(rows, TILE).astype(jnp.float32)))

    def finish_last():
        k, bank = count - 1, last % 2

        def lines(q):
            return pl.ds(edges[q] * nz, (edges[q + 1] - edges[q]) * nz)

        @pl.when(is_inner)
        def _():
            part(jnp.int32(last - (SLOTS - count))).wait_send()
            for q in range(CUTS):
                relay_cut(q).wait_send()
                relay_cut(q).wait_recv()

                def piece(lanes):
                    value = acc[bank, lines(q), lanes] + dot(got.at[2, final, cut(q)], 5, lanes)
                    got[1, final, cut(q), :, lanes] = value.astype(jnp.bfloat16).reshape(-1, nz, TILE)

                tiles(piece)
                part_cut(q).start()

            def store(lanes):
                value = total[bank, :, lanes] - dot(got.at[2, final], 3, lanes)
                dens[k, :, :, lanes] = value.reshape(ny, nz, TILE)

            tiles(store)

        @pl.when(is_outer)
        def _():
            for q in range(CUTS):
                part_cut(q).wait_recv()

                def store(lanes):
                    value = got[2, final, cut(q), :, lanes].reshape(-1, TILE).astype(jnp.float32)
                    dens[k, cut(q), :, lanes] = (total[bank, lines(q), lanes] - value).reshape(-1, nz, TILE)

                tiles(store)

        wait_sent(jnp.int32(last))

    def prepare(i):
        bank = lax.rem(i, 2)
        s, k = i // count, lax.rem(i, count)
        home_sums(i)
        face_y(0, i).wait_recv()
        face_y(1, i).wait_recv()

        @pl.when(k == 0)
        def _():
            face_x(0, s).wait_recv()
            old[1, 1 : ny + 1] = facex[0, s].astype(jnp.float32)

        @pl.when(k < count - 1)
        def _():
            above[...] = dens[k + 1]

        @pl.when(k == count - 1)
        def _():
            face_x(1, s).wait_recv()
            above[...] = facex[1, s].astype(jnp.float32)

        spot = lax.broadcasted_iota(jnp.int32, (nz, 512), 0)
        diagonal = lax.broadcasted_iota(jnp.int32, (nz, nz), 0) == lax.broadcasted_iota(jnp.int32, (nz, nz), 1)
        cur = lax.rem(k, 2)
        old[cur, 1 : ny + 1] = dens[k]
        old[cur, 0] = facey[0, i].astype(jnp.float32) * low_ok
        old[cur, ny + 1] = facey[1, i].astype(jnp.float32) * high_ok

        @pl.loop(0, ny)
        def _(y):
            lit = heat[0, k, pl.ds(y, 1), :].astype(jnp.float32)
            warm = jnp.sum(jnp.where(diagonal, lit, 0.0), axis=1, keepdims=True)
            for lane in range(0, width, 512):
                lanes = slice(lane, lane + 512)
                here = old[cur, y + 1, :, lanes]
                new = rates[0:1, lanes] * here
                new += rates[1:2, lanes] * old[1 - cur, y + 1, :, lanes]
                new += rates[2:3, lanes] * above[y, :, lanes]
                new += rates[3:4, lanes] * old[cur, y, :, lanes]
                new += rates[4:5, lanes] * old[cur, y + 2, :, lanes]
                new += rates[5:6, lanes] * jnp.where(spot == 0, 0.0, pltpu.roll(here, 1, 0))
                new += rates[6:7, lanes] * jnp.where(spot == nz - 1, 0.0, pltpu.roll(here, nz - 1, 0))
                line = pl.ds(pl.multiple_of(y * nz, nz), nz)
                total[bank, line, lanes] = new + warm * rates[7:8, lanes] - total[bank, line, lanes]

    def process(i):
        s, k = i // count, lax.rem(i, count)
        pl.when(i <= count)(lambda: prepare(i))
        near_sums(i)
        pl.when(jnp.logical_and(i >= count, i < last))(lambda: prepare(i + 1))
        pl.when(i < last)(lambda: finish(i))
        pl.when(i == last)(finish_last)
        pl.when(s < STEPS - 1)(lambda: start_new(i + count))

    plane_loads = [pltpu.make_async_copy(phonons.at[0, k], dens.at[k], load_sem.at[4 + k]) for k in range(count)]
    order = (me, inward, jnp.clip(outward, 0, 3), far)
    loads = [
        pltpu.make_async_copy(
            coupling.at[:, pl.ds(pl.multiple_of(block * width, width), width)], weights.at[j], load_sem.at[j]
        )
        for j, block in enumerate(order)
    ]
    barrier = pltpu.get_barrier_semaphore()

    def greet(c, m):
        pl.semaphore_signal(barrier, inc=1, device_id=(c, m), device_id_type=MESH)

    greet(cell, inward)
    pl.when(is_inner)(lambda: greet(cell, outward))
    for c in (y_next, y_last, x_next, x_last, twin) + peers:
        greet(c, me)

    for load in plane_loads:
        load.start()

    small = ((heaters, heat), (courants, courant), (upwinds, upwind), (relaxations, relaxation), (sources, source))
    small_loads = [
        pltpu.make_async_copy(far_ref, near_ref, load_sem.at[4 + count + j]) for j, (far_ref, near_ref) in enumerate(small)
    ]
    def make_rates():
        for load in small_loads:
            load.wait()
        stay = 1.0 - courant[0:1] - courant[1:2] - courant[2:3] - relaxation[...].reshape(1, width)
        rates[0:1] = stay
        for d in range(3):
            speed = courant[d : d + 1]
            forward = upwind[d : d + 1] == 1
            rates[1 + 2 * d : 2 + 2 * d] = jnp.where(forward, speed, 0.0)
            rates[2 + 2 * d : 3 + 2 * d] = jnp.where(forward, 0.0, speed)
        rates[7:8] = source[...].reshape(1, width)

    pl.semaphore_wait(barrier, 9 + inner)

    for i in range(count):
        plane_loads[i].wait()
        own[i] = dens[i].astype(jnp.bfloat16)

        @pl.when(is_inner)
        def _():
            if i < AHEAD[0]:
                own_in(jnp.int32(i)).start()
            own_out(jnp.int32(i)).start()

        start_new(jnp.int32(i))

        if i == 2:
            for load in loads + small_loads:
                load.start()

        if i in LENT_AFTER:
            pl.when(is_outer)(lambda: lent_z(LENT_AFTER.index(i)).start())

    @pl.loop(0, steps_all + 1)
    def _(t):
        @pl.when(is_inner)
        def _():
            @pl.when(t < steps_all)
            def _():
                arrived(1, t)
                pl.when(t < last)(lambda: relay(t).start())

                @pl.when(t == last)
                def _():
                    for q in range(CUTS):
                        relay_cut(q).start()

            pl.when(t + AHEAD[0] < count)(lambda: own_in(t + AHEAD[0]).start())

            @pl.when(jnp.logical_and(t + AHEAD[1] >= count, t + AHEAD[1] < steps_all))
            def _():
                pl.when(t + AHEAD[1] >= SLOTS)(lambda: pl.semaphore_wait(credit, 1))
                own_in(t + AHEAD[1]).start()

            for k in range(3):

                @pl.when(t == PEER_AT[k])
                def _():
                    lent_z(k).wait_recv()
                    for q in range(3):
                        lent_peer(q, k).start()

                @pl.when(t == TWIN_AT[k])
                def _():
                    for q in range(3):
                        lent_peer(q, k).wait_recv()
                    for q in range(4):
                        lent_twin(q, k).start()

                @pl.when(t == READY_AT[k])
                def _():
                    for q in range(4):
                        lent_twin(q, k).wait_recv()

        @pl.when(t == 1)
        def _():
            for load in loads:
                load.wait()
            make_rates()

        @pl.when(t >= 1)
        def _():
            u = t - 1
            process(u)

            @pl.when(jnp.logical_and(is_inner, jnp.logical_and(u >= DRAIN, u < DRAIN + count // 2)))
            def _():
                early_parts(2 * (u - DRAIN))

    @pl.when(is_inner)
    def _():
        for i in range(steps_all - (SLOTS - count), last):
            part(jnp.int32(i)).wait_send()
        for q in range(CUTS):
            part_cut(q).wait_send()
        for k in range(3):
            for q in range(3):
                lent_peer(q, k).wait_send()
            for q in range(4):
                lent_twin(q, k).wait_send()

    @pl.when(is_outer)
    def _():
        for k in range(3):
            lent_z(k).wait_send()


def line_device(phonons, heaters, courant, upwind, relaxation, source, coupling):
    _, count, ny, nz, width = phonons.shape
    calls = STEPS * count
    anywhere, vmem = pl.BlockSpec(memory_space=pl.ANY), pl.BlockSpec(memory_space=pltpu.VMEM)
    dma = pltpu.SemaphoreType.DMA
    half, full = jnp.bfloat16, jnp.float32
    return pl.pallas_call(
        line_kernel,
        out_shape=pltpu.VMEM(phonons.shape, full),
        in_specs=[anywhere] * 7,
        out_specs=vmem,
        scratch_shapes=[
            pltpu.VMEM((ny, nz, width), full),
            pltpu.VMEM((count, ny, nz, width), half),
            pltpu.VMEM((3, SLOTS, ny, nz, width), half),
            pltpu.VMEM((7, width, width), half),
            pltpu.VMEM((2, ny + 2, nz, width), full),
            pltpu.VMEM((2, STEPS, ny, nz, width), half),
            pltpu.VMEM((2, calls, nz, width), half),
            pltpu.VMEM((2, ny * nz, width), full),
            pltpu.VMEM((2, ny * nz, width), full),
            pltpu.VMEM((8, width), full),
            pltpu.VMEM(heaters.shape, heaters.dtype),
            pltpu.VMEM(courant.shape, full),
            pltpu.VMEM(upwind.shape, upwind.dtype),
            pltpu.VMEM(relaxation.shape, full),
            pltpu.VMEM(source.shape, full),
            dma((9 + count,)),
            dma((4, calls)),
            dma((3, calls)),
            dma((2, calls)),
            dma((2, calls)),
            dma((2, STEPS)),
            dma((2, STEPS)),
            dma((24,)),
            dma((24,)),
            dma((2, CUTS)),
            dma((CUTS,)),
            pltpu.SemaphoreType.REGULAR,
        ],
        compiler_params=pltpu.CompilerParams(
            collective_id=0, has_side_effects=True, vmem_limit_bytes=64 * 2**20 - 2**18 - 4 * phonons.size
        ),
    )(phonons, heaters, courant, upwind, relaxation, source, coupling)


def shifted(block, axis, distance):
    devices = range(lax.axis_size(axis))
    route = [((i - distance) % len(devices), i) for i in devices]
    return lax.ppermute(block, axis, route)


def upstream(density, forward, axis):
    widths = [(0, 0)] * density.ndim
    widths[axis] = (1, 1)
    padded = jnp.pad(density, widths)
    length_axis = density.shape[axis]
    behind = lax.slice_in_dim(padded, 0, length_axis, axis=axis)
    ahead = lax.slice_in_dim(padded, 2, length_axis + 2, axis=axis)
    return jnp.where(forward, behind, ahead)


def scatter_term(rounded, coupling):
    contract = (((1,), (1,)), ((), ()))
    gathered = lax.all_gather(rounded, "modes", axis=1, tiled=True)
    return lax.dot_general(gathered, coupling, contract, preferred_element_type=jnp.float32)


def advect(density, courant, upwind, masks):
    lower_y_ok, upper_y_ok = masks
    forward_x = upwind[0] == 1
    forward_y = upwind[1] == 1
    forward_z = upwind[2] == 1
    below_x = shifted(density[-1].astype(jnp.bfloat16), "cells", GY).astype(jnp.float32)
    above_x = shifted(density[0], "cells", -GY)
    below_y = (
        shifted(density[:, -1].astype(jnp.bfloat16), "cells", 1).astype(jnp.float32) * lower_y_ok
    )
    above_y = (
        shifted(density[:, 0].astype(jnp.bfloat16), "cells", -1).astype(jnp.float32) * upper_y_ok
    )
    upstream_z = upstream(density, forward_z, 2)
    transport = courant[0] * (density - upstream(density, forward_x, 0))
    transport = transport + courant[1] * (density - upstream(density, forward_y, 1))
    transport = transport + courant[2] * (density - upstream_z)
    transport = transport.at[0].add(-courant[0] * jnp.where(forward_x, below_x, 0.0))
    transport = transport.at[-1].add(-courant[0] * jnp.where(forward_x, 0.0, above_x))
    transport = transport.at[:, 0].add(-courant[1] * jnp.where(forward_y, below_y, 0.0))
    transport = transport.at[:, -1].add(-courant[1] * jnp.where(forward_y, 0.0, above_y))
    return transport


def per_device(phonons, heaters, courant, upwind, relaxation, source, coupling):
    density = phonons[0]
    cell_count = density.shape[0] * density.shape[1] * density.shape[2]
    mode_count = density.shape[3]
    block_total = lax.axis_size("cells")
    position = (lax.axis_index("cells") + 2) % block_total
    column = position % GY
    masks = ((column != 0).astype(jnp.float32), (column != GY - 1).astype(jnp.float32))
    heating = heaters[0].astype(jnp.float32)[..., None] * source
    for repeat in range(STEPS):
        rounded = density.astype(jnp.bfloat16).reshape(cell_count, mode_count)
        scattered = scatter_term(rounded, coupling).reshape(density.shape)
        transport = advect(density, courant, upwind, masks)
        density = density - transport - relaxation * density - scattered + heating
    return density[None]


def solution(mesh):
    placed = (
        P("cells", None, None, None, "modes"),
        P("cells", None, None, None),
        P(None, "modes"),
        P(None, "modes"),
        P("modes"),
        P("modes"),
        P("modes", None),
    )
    on_line = mesh.shape["modes"] == 4 and mesh.shape["cells"] == 8
    return jax.shard_map(
        line_device if on_line else per_device,
        mesh=mesh,
        in_specs=placed,
        out_specs=P("cells", None, None, None, "modes"),
        check_vma=False,
    )
```
